32 devices in a mesh: grp: 1, deg: 32 (over z, y, x, core).
Axes of the slice: x: 2, y: 2, z: 4, core: 2. Of those that a mesh axis runs over, the one named last changes fastest.
Arguments:
- coeffs_in: float32 [512, 1025, 128], P(('grp', 'deg')), may hold values from -6 to 6
- tables: bfloat16 [512, 1025, 1025], P('deg'), as said below
- order_pairs: int32 [512], replicated, may hold values from 0 to 511, each once
- degree_pairs: int32 [512], replicated, may hold values from 0 to 511, as said below
- angles: float32 [3], replicated, may hold values from -3.140625 to 3.140625
Outputs:
- coeffs_out: float32 [512, 1025, 128], P(('grp', 'deg'))
The draws below stay inside these ranges and needn't reach their ends.
Inputs may be any that keep to these rules, and one draw needn't show every extreme that they name: `order_pairs`: each pair of orders appears once. `degree_pairs`: each pair of degrees appears once. tables[j] is zero outside its two diagonal blocks: the first degree_pairs[j]+1 rows and columns, and the remaining 1024-degree_pairs[j].
All inputs are finite; a program needn't handle non-finite values.
Results may differ from the reference program's by a relative error of at most 0.005.
Values may be sent and summed in bfloat16 or wider, within the bound.
A program may use at most 192 MiB of HBM per device.

```python
import jax
import jax.numpy as jnp
from jax import lax

L = 1024
SH = 64
NPAIR = 512
WIDE = 1025


def pair_permutation(key):
    return jax.random.permutation(jax.random.fold_in(key, 11), NPAIR).astype(jnp.int32)


def draw_degree_pairs(key, part):
    return pair_permutation(key)


def draw_tables(key, part):
    pairs = pair_permutation(key)
    block_low = pairs[:, None, None] + 1
    row_index = jnp.arange(WIDE, dtype=jnp.int32)[None, :, None]
    col_index = jnp.arange(WIDE, dtype=jnp.int32)[None, None, :]
    upper_block = (row_index < block_low) & (col_index < block_low)
    lower_block = (row_index >= block_low) & (col_index >= block_low)
    block_size = jnp.where(row_index < block_low, block_low, WIDE - block_low).astype(jnp.float32)
    raw_values = jax.random.normal(jax.random.fold_in(key, 12), (NPAIR, WIDE, WIDE), jnp.float32)
    scaled = raw_values / jnp.sqrt(block_size)
    return jnp.where(upper_block | lower_block, scaled, 0.0).astype(jnp.bfloat16)


def level_of(stream_key, dims, split, smallest, high):
    gain = 1.0
    for dim, shards_of in split:
        draws = jax.random.uniform(jax.random.fold_in(jax.random.fold_in(stream_key, 6), dim), (shards_of,), jnp.float32, smallest / len(split), high / len(split))
        gain = gain * jnp.repeat(jnp.exp(draws), dims[dim] // shards_of).reshape((-1,) + (1,) * (len(dims) - 1 - dim))
    return gain


def bell_draw(stream_key, extent, deviation, most, cuts=(), kind=jnp.bfloat16):
    array = deviation * jax.random.normal(stream_key, extent, jnp.float32)
    if cuts:
        array = array * level_of(stream_key, extent, cuts, -0.22, 0.18)
    return jnp.clip(array, -most, most).astype(kind)


def setup_inputs(seed: int = 0, part: int = 0) -> dict:
    key_of = jax.random.split(jax.random.key(seed), 6)
    part_keys = jax.random.split(jax.random.fold_in(key_of[5], part), 6)
    coeffs_in = bell_draw(part_keys[0], (NPAIR, WIDE, 2 * SH), 1.0, 6.0, ((0, 32),), jnp.float32)
    tables = draw_tables(jax.random.fold_in(key_of[5], 71), part)
    order_pairs = jax.random.permutation(key_of[2], NPAIR).astype(jnp.int32)
    degree_pairs = draw_degree_pairs(jax.random.fold_in(key_of[5], 71), part)
    angles = jnp.clip(jax.random.uniform(key_of[4], (3,), jnp.float32, -3.140625, 3.140625), -3.140625, 3.140625)
    return dict(coeffs_in=coeffs_in, tables=tables, order_pairs=order_pairs, degree_pairs=degree_pairs, angles=angles)


def rotate_phase(values, order_map, angle):
    half = values.shape[-1] // 2
    turn = order_map.astype(jnp.float32)[..., None] * angle
    cosine = jnp.cos(turn)
    sine_part = jnp.sin(turn)
    real_part = values[..., :half].astype(jnp.float32)
    imag_part = values[..., half:].astype(jnp.float32)
    return jnp.concatenate([real_part * cosine + imag_part * sine_part, imag_part * cosine - real_part * sine_part], -1)


def reference(coeffs_in, tables, order_pairs, degree_pairs, angles):
    top = L
    position = jnp.arange(WIDE, dtype=jnp.int32)[None, :]
    order_low = order_pairs.astype(jnp.int32)[:, None]
    order_map = jnp.where(position < top - order_low, order_low, top - 1 - order_low)
    turned = rotate_phase(coeffs_in, order_map, angles[2]).astype(jnp.bfloat16)
    counting = jnp.arange(NPAIR, dtype=jnp.int32)
    inverse_order = jnp.zeros((NPAIR,), jnp.int32).at[order_pairs].set(counting)
    inverse_degree = jnp.zeros((NPAIR,), jnp.int32).at[degree_pairs].set(counting)
    degree_low = degree_pairs.astype(jnp.int32)[:, None]
    lower_part = position <= degree_low
    degree_full = jnp.where(lower_part, degree_low, top - 1 - degree_low)
    degree_map = jnp.where(lower_part, position, position - degree_low - 1)
    low_order = degree_map < NPAIR
    order_base = jnp.where(low_order, degree_map, top - 1 - degree_map)
    source_row = inverse_order[order_base]
    source_pos = jnp.where(low_order, degree_full - order_base, (top - order_base) + (degree_full - degree_map))
    by_degree = turned[source_row, source_pos]
    tilt = angles[1]

    def one_pair(packed):
        table, block, pair_orders = packed
        first_pass = jnp.dot(table, block, preferred_element_type=jnp.float32)
        tilted = rotate_phase(first_pass, pair_orders, tilt).astype(jnp.bfloat16)
        return jnp.dot(table, tilted, preferred_element_type=jnp.float32).astype(jnp.bfloat16)

    second = lax.map(one_pair, (tables, by_degree, degree_map))
    high_part = position >= top - order_low
    degree_back = jnp.where(high_part, position - 1, order_low + position)
    low_degree = degree_back < NPAIR
    pair_base = jnp.where(low_degree, degree_back, top - 1 - degree_back)
    target_pos = jnp.where(low_degree, order_map, pair_base + 1 + order_map)
    target_row = inverse_degree[pair_base]
    gathered = second[target_row, target_pos]
    return rotate_phase(gathered, order_map, angles[0])
```

```python
import functools

import jax
import jax.numpy as jnp
from jax import lax
from jax.experimental import pallas as pl
from jax.experimental.pallas import tpu as pltpu
from jax.sharding import PartitionSpec as P


def rotate_phase(values, order_map, angle):
    half = values.shape[-1] // 2
    turn = order_map.astype(jnp.float32)[..., None] * angle
    cosine = jnp.cos(turn)
    sine_part = jnp.sin(turn)
    real_part = values[..., :half].astype(jnp.float32)
    imag_part = values[..., half:].astype(jnp.float32)
    return jnp.concatenate(
        [real_part * cosine + imag_part * sine_part, imag_part * cosine - real_part * sine_part], -1
    )


def packed_places(order_low, degree_low, top):
    lower_side = order_low <= degree_low
    order_pos = jnp.stack(
        [
            top - 1 - degree_low - order_low,
            jnp.where(lower_side, degree_low - order_low, top - degree_low),
        ],
        -1,
    )
    degree_pos = jnp.stack(
        [
            degree_low + 1 + order_low,
            jnp.where(lower_side, order_low, top + degree_low - order_low),
        ],
        -1,
    )
    return (order_pos, degree_pos)


def indicator(places, alive, width):
    columns = jnp.arange(width, dtype=jnp.int32)
    return ((places[..., None] == columns) & alive[..., None]).astype(jnp.bfloat16)


def gather_slots(form, source, places, alive):
    width = source.shape[1]
    pieces = []
    for slot in range(places.shape[-1]):
        table = indicator(places[..., slot], alive[..., slot], width)
        pieces.append(
            jnp.einsum(form, table, source, preferred_element_type=jnp.float32).astype(jnp.bfloat16)
        )
    return jnp.stack(pieces, -2)


def place_slots(form, values, places, alive, width):
    total = None
    for slot in range(places.shape[-1]):
        table = indicator(places[..., slot], alive[..., slot], width)
        term = jnp.einsum(form, table, values[..., slot, :], preferred_element_type=jnp.float32)
        total = term if total is None else total + term
    return total.astype(jnp.bfloat16)


def transform(tables, by_degree, degree_map, tilt):
    first_pass = jnp.einsum("jab,jbc->jac", tables, by_degree, preferred_element_type=jnp.float32)
    tilted = rotate_phase(first_pass, degree_map, tilt).astype(jnp.bfloat16)
    second = jnp.einsum("jab,jbc->jac", tables, tilted, preferred_element_type=jnp.float32)
    return second.astype(jnp.bfloat16)


def small_shards(coeffs_in, tables, order_pairs, degree_pairs, angles):
    local_pairs, width, channels = coeffs_in.shape
    top = width - 1
    devices = lax.axis_size("deg")
    device = lax.axis_index("deg")
    my_orders = lax.dynamic_slice_in_dim(order_pairs, device * local_pairs, local_pairs)
    my_degrees = lax.dynamic_slice_in_dim(degree_pairs, device * local_pairs, local_pairs)
    all_orders = order_pairs.reshape(devices, local_pairs)
    all_degrees = degree_pairs.reshape(devices, local_pairs)
    position = jnp.arange(width, dtype=jnp.int32)[None, :]
    order_map = jnp.where(
        position < top - my_orders[:, None], my_orders[:, None], top - 1 - my_orders[:, None]
    )
    degree_map = jnp.where(
        position <= my_degrees[:, None], position, position - my_degrees[:, None] - 1
    )
    turned = rotate_phase(coeffs_in, order_map, angles[2]).astype(jnp.bfloat16)
    grid_shape = (devices, local_pairs, local_pairs)
    outward_orders = jnp.broadcast_to(my_orders[None, :, None], grid_shape)
    outward_degrees = jnp.broadcast_to(all_degrees[:, None, :], grid_shape)
    inward_orders = jnp.broadcast_to(all_orders[:, :, None], grid_shape)
    inward_degrees = jnp.broadcast_to(my_degrees[None, None, :], grid_shape)
    out_opos, out_dpos = packed_places(outward_orders, outward_degrees, top)
    in_opos, in_dpos = packed_places(inward_orders, inward_degrees, top)
    out_alive = jnp.ones(out_opos.shape, jnp.bool_)
    in_alive = jnp.ones(in_dpos.shape, jnp.bool_)
    out_found = jnp.any(outward_degrees == outward_orders, axis=-1)
    in_match = inward_degrees == inward_orders
    in_found = jnp.any(in_match, axis=-1)
    in_choice = jnp.argmax(in_match.astype(jnp.int32), axis=-1)
    degree_rows = jnp.arange(local_pairs, dtype=jnp.int32)
    matching = ((in_choice[..., None] == degree_rows) & in_found[..., None]).astype(jnp.bfloat16)
    row_found = jnp.any((in_choice[..., None] == degree_rows) & in_found[..., None], axis=(0, 1))
    extra_places = top - my_orders
    extra_values = jnp.take_along_axis(turned, extra_places[:, None, None], 1)[:, 0]
    main_send = gather_slots("drcw,rwx->drcx", turned, out_opos, out_alive)
    extra_send = jnp.where(out_found[..., None], extra_values[None], 0)
    main_arrived, extra_arrived = (
        lax.all_to_all(main_send, "deg", split_axis=0, concat_axis=0, tiled=True),
        lax.all_to_all(extra_send, "deg", split_axis=0, concat_axis=0, tiled=True),
    )
    by_degree = place_slots("drcw,drcx->cwx", main_arrived, in_dpos, in_alive, width)
    extra_column = jnp.einsum(
        "drq,drx->qx", matching, extra_arrived, preferred_element_type=jnp.float32
    ).astype(jnp.bfloat16)
    by_degree = by_degree.at[:, top].set(
        jnp.where(row_found[:, None], extra_column, by_degree[:, top])
    )
    second = transform(tables, by_degree, degree_map, angles[1])
    main_back = gather_slots("drcw,cwx->drcx", second, in_dpos, in_alive)
    extra_back = jnp.einsum(
        "drq,qx->drx", matching, second[:, top], preferred_element_type=jnp.float32
    ).astype(jnp.bfloat16)
    main_home, extra_home = (
        lax.all_to_all(main_back, "deg", split_axis=0, concat_axis=0, tiled=True),
        lax.all_to_all(extra_back, "deg", split_axis=0, concat_axis=0, tiled=True),
    )
    by_order = place_slots("drcw,drcx->rwx", main_home, out_opos, out_alive, width)
    home_values = jnp.sum(
        jnp.where(out_found[..., None], extra_home.astype(jnp.float32), 0.0), axis=0
    ).astype(jnp.bfloat16)
    home_found = jnp.any(out_found, axis=0)
    home_mask = (position == extra_places[:, None]) & home_found[:, None]
    by_order = jnp.where(home_mask[..., None], home_values[:, None, :], by_order)
    return rotate_phase(by_order, order_map, angles[0])


VMEM = pl.BlockSpec(memory_space=pltpu.VMEM)
SMEM = pl.BlockSpec(memory_space=pltpu.SMEM)
ANY = pl.BlockSpec(memory_space=pl.ANY)
MESH = pl.DeviceIdType.MESH
F32 = jnp.float32
BF16 = jnp.bfloat16
HALF = 8
EACH = 4
SLAB = 32


def onehot(a, b):
    return jnp.where(a == b, 1.0, 0.0)


def rotate(v, cosine, sine):
    return v * cosine + pltpu.roll(v, v.shape[-1] // 2, v.ndim - 1) * sine


def dot(a, b):
    return jnp.dot(a, b, preferred_element_type=F32)


def iota(shape, dim):
    return lax.broadcasted_iota(jnp.int32, shape, dim)


def lows(orders):
    shape = (len(orders), 128)
    low = jnp.zeros(shape, jnp.int32)
    for r, order in enumerate(orders):
        low = jnp.where(iota(shape, 0) == r, order, low)
    return low


def phase(order, angle):
    turn = order.astype(F32) * angle
    sine = jnp.sin(turn)
    return jnp.cos(turn), jnp.where(iota(turn.shape, 1) < 64, sine, -sine)


def turning(low, angle, top):
    return [t for order in (low, top - 1 - low) for t in phase(order, angle)]


def fused_kernel(
    n, local, pairs,
    ord_s, deg_s, ang_s, x_ref, raw_ref, qrow, prow,
    rows_out, tab_ref,
    send, recv, back, home, xs, line, scr0, scr1, mats, tbuf, raw, slab, stage,
    uv, xb, sb, ct, st, cs, extra, ebuf, eall, last, lbuf, lall, exb, orow,
    out_s, out_r, bk_s, bk_r, ex_s, ex_r, loc, xsem, rawsem, stsem, tsem, osem,
):
    me = lax.axis_index("deg")
    top = 2 * pairs
    width = top + 1
    deep = xb.shape[0]
    span = local * HALF
    chunks = local // EACH
    lead = line.shape[1] - deep

    def peer_of(i):
        step = lax.div(i, 2) + (n // 2) * lax.rem(i, 2)
        return lax.rem(me + step, n)

    barrier = pltpu.get_barrier_semaphore()

    def greet(i, carry):
        pl.semaphore_signal(
            barrier, inc=1, device_id={"deg": lax.rem(me + i, n)}, device_id_type=MESH
        )
        return carry

    lax.fori_loop(1, n, greet, 0)

    def fetch_x(h):
        return pltpu.make_async_copy(
            x_ref.at[:, pl.ds(h * HALF, HALF), :], xs.at[h], xsem.at[h]
        )

    def fetch_raw(b, slot):
        return pltpu.make_async_copy(
            raw_ref.at[pl.ds(b * SLAB, SLAB)], raw.at[slot], rawsem.at[slot]
        )

    fetch_x(0).start()
    fetch_x(1).start()
    fetch_raw(0, 0).start()

    def pushing(src, dst, at, count, h, ssem, rsem, i):
        peer = peer_of(i)
        return pltpu.make_async_remote_copy(
            src_ref=src.at[h, peer, pl.ds(at, count)],
            dst_ref=dst.at[h, me, pl.ds(at, count)],
            send_sem=ssem, recv_sem=rsem, device_id={"deg": peer}, device_id_type=MESH,
        )

    def push(src, dst, k, h, ssem, rsem):
        def one(i, carry):
            pushing(src, dst, k * EACH, EACH, h, ssem, rsem, i).start()
            return carry

        lax.fori_loop(1, n, one, 0)

    def whole(src, dst, k, h, ssem, rsem):
        part = (h, pl.ds(0, n - 1), pl.ds(k * EACH, EACH))
        return pltpu.make_async_remote_copy(
            src_ref=src.at[part], dst_ref=dst.at[part],
            send_sem=ssem, recv_sem=rsem, device_id={"deg": lax.rem(me + 1, n)}, device_id_type=MESH,
        )

    def spread(src, dst, s):
        def one(i, carry):
            pltpu.make_async_remote_copy(
                src_ref=src, dst_ref=dst.at[me], send_sem=ex_s.at[s], recv_sem=ex_r.at[s],
                device_id={"deg": peer_of(i)}, device_id_type=MESH,
            ).start()
            return carry

        lax.fori_loop(1, n, one, 0)

    def spread_all(dst, s):
        part = dst.at[pl.ds(0, n - 1)]
        return pltpu.make_async_remote_copy(
            src_ref=part, dst_ref=part, send_sem=ex_s.at[s], recv_sem=ex_r.at[s],
            device_id={"deg": lax.rem(me + 1, n)}, device_id_type=MESH,
        )

    def push_out(p):
        k, h = lax.div(p, 2), lax.rem(p, 2)
        push(send, recv, k, h, out_s.at[p], out_r.at[p])

    def stay(src, dst, h, s):
        return pltpu.make_async_copy(src.at[h, me], dst.at[h, me], loc.at[s])

    level = iota((pairs, pairs), 0)
    mats[0] = onehot(pairs - 1 - level, qrow[...]).T.astype(BF16)
    mats[1] = onehot(level, qrow[...]).T.astype(BF16)
    my_lows = lows([ord_s[me * local + r] for r in range(local)])
    for i, t in enumerate(turning(my_lows, ang_s[2], top)):
        cs[i] = t
    row = iota((pairs, 1), 0)

    def pack(h):
        flat = xs.at[h].reshape(width * HALF, 128)

        def one(r, slot):
            at = h * HALF + r
            p = ord_s[me * local + at]
            cl, sl, ch, sh = (cs[i, pl.ds(at, 1), :] for i in range(4))
            line[slot, lead : lead + width, :] = flat[pl.ds(r, width, stride=HALF), :]

            def load(pos):
                return line[slot, pl.ds(lead + pos, pairs), :]

            low = jnp.where(row >= p, rotate(load(-p), cl, sl), 0.0).astype(BF16)
            mid = rotate(load(pairs - p), cl, sl).astype(BF16)
            high = jnp.where(row >= pairs - p, rotate(load(pairs + 1), ch, sh), 0.0).astype(BF16)
            both = dot(mats[0], jnp.concatenate([mid, high], 1))
            extra[pl.ds(at, 1), :] = rotate(line[slot, pl.ds(lead + top - p, 1), :], ch, sh)
            return low, both

        def step(i, carry):
            r = 2 * i
            low_a, both_a = one(r, 0)
            low_b, both_b = one(r + 1, 1)
            both_low = dot(mats[1], jnp.concatenate([low_a, low_b], 1))
            for at, both, low in ((r, both_a, both_low[:, :128]), (r + 1, both_b, both_low[:, 128:])):
                scr0[pl.ds(at, pairs, stride=HALF), :] = both[:, :128]
                scr1[pl.ds(at, pairs, stride=HALF), :] = both[:, 128:] + low
            return carry

        lax.fori_loop(0, HALF // 2, step, 0)

        def emit(d, carry):
            at = pl.multiple_of(d * span, 8)
            v0 = scr0[pl.ds(at, span), :].reshape(local, HALF, 128)
            v1 = scr1[pl.ds(at, span), :].reshape(local, HALF, 128)
            send[h, d] = jnp.concatenate([v0, v1], 1).astype(BF16)
            return carry

        lax.fori_loop(0, n, emit, 0)

    fetch_x(0).wait()
    pack(0)
    pl.semaphore_wait(barrier, n - 1)
    push_out(0)
    stay(send, recv, 0, 0).start()
    fetch_x(1).wait()
    pack(1)
    push_out(1)
    stay(send, recv, 1, 1).start()
    ebuf[...] = extra[...].astype(BF16)
    eall[me] = ebuf[...]
    spread(ebuf, eall, 0)
    push_out(2)

    slabs = top // SLAB

    def store_slab(b, slot):
        return pltpu.make_async_copy(
            stage.at[slot], tab_ref.at[:, pl.ds(pl.multiple_of(b * SLAB, SLAB), SLAB), :], stsem.at[slot]
        )

    def turn_slab(b, carry):
        slot = lax.rem(b, 2)

        @pl.when(b + 1 < slabs)
        def _():
            fetch_raw(b + 1, 1 - slot).start()

        fetch_raw(b, slot).wait()

        @pl.when(b >= 2)
        def _():
            store_slab(b - 2, slot).wait()

        for t in range(slab.shape[0]):
            lanes = slice(t * 128, min(t * 128 + 128, width))
            wide = lanes.stop - lanes.start
            slab[t, :, 0:wide] = raw[slot, :, :, lanes].astype(F32).reshape(SLAB * local, wide)
            for j in range(local):
                got = slab.at[t][pl.ds(j, SLAB, stride=local), :]
                stage[slot, j, :, lanes] = got[:, :wide].astype(BF16)
        store_slab(b, slot).start()

        @pl.when(b == slabs // 2)
        def _():
            push_out(3)

        return carry

    lax.fori_loop(0, slabs, turn_slab, 0)
    push_out(4)
    end = pltpu.make_async_copy(raw_ref.at[pl.ds(top, 1)], raw.at[0, pl.ds(0, 1)], rawsem.at[0])
    end.start()
    store_slab(slabs - 2, 0).wait()
    end.wait()
    edge = raw[0, 0].astype(F32)
    first_row = iota((16, 1), 0) == 0
    for j in range(local):
        stage[0, j, 0:16, :] = jnp.where(first_row, edge[j : j + 1, :], 0.0).astype(BF16)
    end = pltpu.make_async_copy(stage.at[0, :, pl.ds(0, 16), :], tab_ref.at[:, pl.ds(top, 16), :], stsem.at[0])
    end.start()
    store_slab(slabs - 1, 1).wait()
    end.wait()

    def fetch_table(c, slot):
        return pltpu.make_async_copy(tab_ref.at[c], tbuf.at[slot], tsem.at[slot])

    fetch_table(0, 0).start()
    a0 = onehot(level, prow[...])
    arev = onehot(pairs - 1 - level, prow[...])
    mats[2] = a0.astype(BF16)
    mats[3] = arev.astype(BF16)
    mats[4] = a0.T.astype(BF16)
    mats[5] = arev.T.astype(BF16)

    def tilt(b, carry):
        at = pl.multiple_of(b * 16, 16)
        cosine, sine = phase(at - pairs + iota((16, 128), 0), ang_s[1])
        ct[pl.ds(at, 16), :] = cosine
        st[pl.ds(at, 16), :] = sine
        return carry

    lax.fori_loop(0, ct.shape[0] // 16, tilt, 0)
    for h in range(2):
        stay(send, recv, h, h).wait()
    spread_all(eall, 0).wait_recv()

    def degree(c, carry):
        slot = lax.rem(c, 2)
        k = lax.div(c, EACH)
        spot = lax.rem(c, EACH)

        @pl.when(c + 1 < local)
        def _():
            fetch_table(c + 1, 1 - slot).start()

        @pl.when(spot == 0)
        def _():
            for h in range(2):
                p = 2 * k + h
                whole(send, recv, k, h, out_s.at[p], out_r.at[p]).wait_recv()

        q = deg_s[me * local + c]
        x0 = recv[0, :, c].astype(F32)
        x1 = recv[1, :, c].astype(F32)
        in0 = jnp.concatenate([x0[:, :HALF], x1[:, :HALF]], 1).reshape(pairs, 128).astype(BF16)
        in1 = jnp.concatenate([x0[:, HALF:], x1[:, HALF:]], 1).reshape(pairs, 128).astype(BF16)
        u = dot(mats[2], jnp.concatenate([in0, in1], 1))
        v = dot(mats[3], in1)
        uv[pairs : 2 * pairs, :] = u[:, :128]
        uv[2 * pairs : 3 * pairs, :] = v
        pick = onehot(jnp.broadcast_to(prow[...], (16, pairs)), q).astype(BF16)
        e = dot(pick, eall[...].reshape(pairs, 128))
        xb[0:pairs, :] = jnp.where(row <= q, u[:, 128:], uv[pl.ds(pairs - 1 - q, pairs), :]).astype(BF16)
        xb[pairs:top, :] = uv[pl.ds(top - 1 - q, pairs), :].astype(BF16)
        xb[top : top + 16, :] = e.astype(BF16)
        fetch_table(c, slot).wait()
        first = dot(tbuf[slot], xb[0:width, :])
        low = iota((deep, 1), 0) <= q
        cosine = jnp.where(low, ct[pairs : pairs + deep, :], ct[pl.ds(pairs - 1 - q, deep), :])
        sine = jnp.where(low, st[pairs : pairs + deep, :], st[pl.ds(pairs - 1 - q, deep), :])
        xb[...] = rotate(first, cosine, sine).astype(BF16)
        sb[0:deep, :] = dot(tbuf[slot], xb[0:width, :]).astype(BF16).astype(F32)
        f0 = sb[pl.ds(q + 1, pairs), :].astype(BF16)
        f1 = jnp.where(row <= q, sb[0:pairs, :], 0.0).astype(BF16)
        f2 = jnp.where(row < pairs - 1 - q, sb[pl.ds(q + 1 + pairs, pairs), :], 0.0).astype(BF16)
        g = dot(mats[4], jnp.concatenate([f0, f1], 1))
        g0 = g[:, :128].reshape(n, local, 128)
        g1 = (g[:, 128:] + dot(mats[5], f2)).reshape(n, local, 128)
        for h in range(2):
            cut = slice(h * HALF, (h + 1) * HALF)
            back[h, :, c] = jnp.concatenate([g0[:, cut], g1[:, cut]], 1).astype(BF16)
        last[pl.ds(c, 1), :] = sb[top : top + 1, :]

        @pl.when((lax.rem(c, 2) == 1) & (c < 6))
        def _():
            push_out(5 + lax.div(c, 2))

        @pl.when(spot == EACH - 1)
        def _():
            for h in range(2):
                p = 2 * k + h
                push(back, home, k, h, bk_s.at[p], bk_r.at[p])

        return carry

    lax.fori_loop(0, local, degree, 0)
    lbuf[...] = last[...].astype(BF16)
    lall[me] = lbuf[...]
    spread(lbuf, lall, 1)
    for h in range(2):
        stay(back, home, h, 2 + h).start()
    mats[0] = onehot(pairs - 1 - level, qrow[...]).astype(BF16)
    mats[1] = onehot(level, qrow[...]).astype(BF16)
    spread_all(lall, 1).wait_recv()
    mine = onehot(jnp.broadcast_to(my_lows[:, :1], (local, pairs)), qrow[...]).astype(BF16)
    exb[...] = dot(mine, lall[...].reshape(pairs, 128))
    place = iota((deep, 1), 0)

    def store_row(j, slot):
        return pltpu.make_async_copy(orow.at[slot], rows_out.at[j], osem.at[slot])

    for h in range(2):
        for k in range(chunks):
            p = 2 * k + h
            whole(back, home, k, h, bk_s.at[p], bk_r.at[p]).wait_recv()
        stay(back, home, h, 2 + h).wait()

        def take(d, carry):
            at = pl.multiple_of(d * span, 8)
            got = home[h, d].astype(F32)
            scr0[pl.ds(at, span), :] = got[:, :HALF].reshape(span, 128)
            scr1[pl.ds(at, span), :] = got[:, HALF:].reshape(span, 128)
            return carry

        lax.fori_loop(0, n, take, 0)

        def step(i, carry):
            r = 2 * i
            s1s, boths = [], []
            for at in (r, r + 1):
                s0 = scr0[pl.ds(at, pairs, stride=HALF), :].astype(BF16)
                s1 = scr1[pl.ds(at, pairs, stride=HALF), :].astype(BF16)
                s1s.append(s1)
                boths.append(dot(mats[0], jnp.concatenate([s0, s1], 1)))
            both_low = dot(mats[1], jnp.concatenate(s1s, 1))
            for s, both in enumerate(boths):
                j = h * HALF + r + s
                p = ord_s[me * local + j]
                line[s, 0:pairs, :] = both_low[:, s * 128 : (s + 1) * 128]
                line[s, pairs:top, :] = both[:, :128]
                sb[pairs + 1 : top + 1, :] = both[:, 128:]
                if h == 1:
                    store_row(j - 2, s).wait()
                else:
                    @pl.when(i > 0)
                    def _():
                        store_row(j - 2, s).wait()
                value = jnp.where(place == top - p, exb[pl.ds(j, 1), :], sb[0:deep, :])
                orow[s] = jnp.where(place < top - p, line[s, pl.ds(p, deep), :], value).astype(BF16)
                store_row(j, s).start()
            return carry

        lax.fori_loop(0, HALF // 2, step, 0)
    for s in range(2):
        store_row(local - 2 + s, s).wait()
    for p in range(2 * chunks):
        whole(send, recv, p // 2, p % 2, out_s.at[p], out_r.at[p]).wait_send()
        whole(back, home, p // 2, p % 2, bk_s.at[p], bk_r.at[p]).wait_send()
    spread_all(eall, 0).wait_send()
    spread_all(lall, 1).wait_send()


def finish_kernel(local, top, ord_s, ang_s, in_ref, out_ref, cs):
    block = pl.program_id(0)
    start = lax.axis_index("deg") * local
    size = out_ref.shape[0]

    @pl.when(block == 0)
    def _():
        for i, t in enumerate(turning(lows([ord_s[start + r] for r in range(local)]), ang_s[0], top)):
            cs[i] = t

    place = block * size + iota((size, 1), 0)
    flat = out_ref.reshape(size * local, 128)
    for r in range(local):
        low = place < top - ord_s[start + r]
        cosine = jnp.where(low, cs[0, r : r + 1, :], cs[2, r : r + 1, :])
        sine = jnp.where(low, cs[1, r : r + 1, :], cs[3, r : r + 1, :])
        flat[pl.ds(r, size, stride=local), :] = rotate(in_ref[r].astype(F32), cosine, sine)


def shards(coeffs_in, tables, order_pairs, degree_pairs, angles):
    local, width, channels = coeffs_in.shape
    top = width - 1
    pairs = top // 2
    if local != 2 * HALF or channels != 128 or pairs % 128:
        return small_shards(coeffs_in, tables, order_pairs, degree_pairs, angles)
    n = lax.axis_size("deg")
    deep = top + 16
    chunks = local // EACH
    standing = jnp.transpose(coeffs_in, (1, 0, 2))
    tables = jnp.transpose(tables, (1, 0, 2))
    wire = pltpu.VMEM((2, n, local, 2 * HALF, 128), BF16)
    small = pltpu.VMEM((local, 128), F32)
    small16 = pltpu.VMEM((local, 128), BF16)
    every = pltpu.VMEM((n, local, 128), BF16)
    sems = lambda count: pltpu.SemaphoreType.DMA((count,))
    by_row, _ = pl.pallas_call(
        functools.partial(fused_kernel, n, local, pairs),
        name="fused",
        out_shape=[
            jax.ShapeDtypeStruct((local, deep, 128), BF16),
            jax.ShapeDtypeStruct((local, deep, width), BF16),
        ],
        in_specs=[SMEM, SMEM, SMEM, ANY, ANY, VMEM, VMEM],
        out_specs=[ANY, ANY],
        scratch_shapes=[
            wire, wire, wire, wire,
            pltpu.VMEM((2, width, HALF, 128), F32),
            pltpu.VMEM((2, pairs + deep, 128), F32),
            pltpu.VMEM((pairs * HALF, 128), F32),
            pltpu.VMEM((pairs * HALF, 128), F32),
            pltpu.VMEM((6, pairs, pairs), BF16),
            pltpu.VMEM((2, deep, width), BF16),
            pltpu.VMEM((2, SLAB, local, width), BF16),
            pltpu.VMEM((pl.cdiv(width, 128), SLAB * local, 128), F32),
            pltpu.VMEM((2, local, SLAB, width), BF16),
            pltpu.VMEM((3 * pairs, 128), F32),
            pltpu.VMEM((deep, 128), BF16),
            pltpu.VMEM((3 * pairs, 128), F32),
            pltpu.VMEM((pairs + deep, 128), F32),
            pltpu.VMEM((pairs + deep, 128), F32),
            pltpu.VMEM((4, local, 128), F32),
            small, small16, every, small, small16, every, small,
            pltpu.VMEM((2, deep, 128), BF16),
            sems(2 * chunks), sems(2 * chunks), sems(2 * chunks), sems(2 * chunks),
            sems(2), sems(2), sems(4), sems(2), sems(2), sems(2), sems(2), sems(2),
        ],
        compiler_params=pltpu.CompilerParams(
            collective_id=0, has_side_effects=True, vmem_limit_bytes=60 * 1024 * 1024
        ),
    )(order_pairs, degree_pairs, angles, standing, tables, degree_pairs[None, :], order_pairs[None, :])
    size = 208
    result = pl.pallas_call(
        functools.partial(finish_kernel, local, top),
        name="finish",
        out_shape=jax.ShapeDtypeStruct((width, local, 128), F32),
        grid=(pl.cdiv(width, size),),
        in_specs=[SMEM, SMEM, pl.BlockSpec((local, size, 128), lambda b: (0, b, 0))],
        out_specs=pl.BlockSpec((size, local, 128), lambda b: (b, 0, 0)),
        scratch_shapes=[pltpu.VMEM((4, local, 128), F32)],
    )(order_pairs, angles, by_row)
    return jnp.transpose(result, (1, 0, 2))


def solution(mesh):
    return jax.shard_map(
        shards,
        mesh=mesh,
        in_specs=(P(("grp", "deg"), None, None), P("deg", None, None), P(), P(), P()),
        out_specs=P(("grp", "deg"), None, None),
        check_vma=False,
    )
```

```python
import functools

import jax
import jax.numpy as jnp
from jax import lax
from jax.experimental import pallas as pl
from jax.experimental.pallas import tpu as pltpu
from jax.sharding import PartitionSpec as P


def rotate_phase(values, order_map, angle):
    half = values.shape[-1] // 2
    turn = order_map.astype(jnp.float32)[..., None] * angle
    cosine = jnp.cos(turn)
    sine_part = jnp.sin(turn)
    real_part = values[..., :half].astype(jnp.float32)
    imag_part = values[..., half:].astype(jnp.float32)
    return jnp.concatenate(
        [real_part * cosine + imag_part * sine_part, imag_part * cosine - real_part * sine_part], -1
    )


def packed_places(order_low, degree_low, top):
    lower_side = order_low <= degree_low
    order_pos = jnp.stack(
        [
            top - 1 - degree_low - order_low,
            jnp.where(lower_side, degree_low - order_low, top - degree_low),
        ],
        -1,
    )
    degree_pos = jnp.stack(
        [
            degree_low + 1 + order_low,
            jnp.where(lower_side, order_low, top + degree_low - order_low),
        ],
        -1,
    )
    return (order_pos, degree_pos)


def indicator(places, alive, width):
    columns = jnp.arange(width, dtype=jnp.int32)
    return ((places[..., None] == columns) & alive[..., None]).astype(jnp.bfloat16)


def gather_slots(form, source, places, alive):
    width = source.shape[1]
    pieces = []
    for slot in range(places.shape[-1]):
        table = indicator(places[..., slot], alive[..., slot], width)
        pieces.append(
            jnp.einsum(form, table, source, preferred_element_type=jnp.float32).astype(jnp.bfloat16)
        )
    return jnp.stack(pieces, -2)


def place_slots(form, values, places, alive, width):
    total = None
    for slot in range(places.shape[-1]):
        table = indicator(places[..., slot], alive[..., slot], width)
        term = jnp.einsum(form, table, values[..., slot, :], preferred_element_type=jnp.float32)
        total = term if total is None else total + term
    return total.astype(jnp.bfloat16)


def transform(tables, by_degree, degree_map, tilt):
    first_pass = jnp.einsum("jab,jbc->jac", tables, by_degree, preferred_element_type=jnp.float32)
    tilted = rotate_phase(first_pass, degree_map, tilt).astype(jnp.bfloat16)
    second = jnp.einsum("jab,jbc->jac", tables, tilted, preferred_element_type=jnp.float32)
    return second.astype(jnp.bfloat16)


def small_shards(coeffs_in, tables, order_pairs, degree_pairs, angles):
    local_pairs, width, channels = coeffs_in.shape
    top = width - 1
    devices = lax.axis_size("deg")
    device = lax.axis_index("deg")
    my_orders = lax.dynamic_slice_in_dim(order_pairs, device * local_pairs, local_pairs)
    my_degrees = lax.dynamic_slice_in_dim(degree_pairs, device * local_pairs, local_pairs)
    all_orders = order_pairs.reshape(devices, local_pairs)
    all_degrees = degree_pairs.reshape(devices, local_pairs)
    position = jnp.arange(width, dtype=jnp.int32)[None, :]
    order_map = jnp.where(
        position < top - my_orders[:, None], my_orders[:, None], top - 1 - my_orders[:, None]
    )
    degree_map = jnp.where(
        position <= my_degrees[:, None], position, position - my_degrees[:, None] - 1
    )
    turned = rotate_phase(coeffs_in, order_map, angles[2]).astype(jnp.bfloat16)
    grid_shape = (devices, local_pairs, local_pairs)
    outward_orders = jnp.broadcast_to(my_orders[None, :, None], grid_shape)
    outward_degrees = jnp.broadcast_to(all_degrees[:, None, :], grid_shape)
    inward_orders = jnp.broadcast_to(all_orders[:, :, None], grid_shape)
    inward_degrees = jnp.broadcast_to(my_degrees[None, None, :], grid_shape)
    out_opos, out_dpos = packed_places(outward_orders, outward_degrees, top)
    in_opos, in_dpos = packed_places(inward_orders, inward_degrees, top)
    out_alive = jnp.ones(out_opos.shape, jnp.bool_)
    in_alive = jnp.ones(in_dpos.shape, jnp.bool_)
    out_found = jnp.any(outward_degrees == outward_orders, axis=-1)
    in_match = inward_degrees == inward_orders
    in_found = jnp.any(in_match, axis=-1)
    in_choice = jnp.argmax(in_match.astype(jnp.int32), axis=-1)
    degree_rows = jnp.arange(local_pairs, dtype=jnp.int32)
    matching = ((in_choice[..., None] == degree_rows) & in_found[..., None]).astype(jnp.bfloat16)
    row_found = jnp.any((in_choice[..., None] == degree_rows) & in_found[..., None], axis=(0, 1))
    extra_places = top - my_orders
    extra_values = jnp.take_along_axis(turned, extra_places[:, None, None], 1)[:, 0]
    main_send = gather_slots("drcw,rwx->drcx", turned, out_opos, out_alive)
    extra_send = jnp.where(out_found[..., None], extra_values[None], 0)
    main_arrived, extra_arrived = (
        lax.all_to_all(main_send, "deg", split_axis=0, concat_axis=0, tiled=True),
        lax.all_to_all(extra_send, "deg", split_axis=0, concat_axis=0, tiled=True),
    )
    by_degree = place_slots("drcw,drcx->cwx", main_arrived, in_dpos, in_alive, width)
    extra_column = jnp.einsum(
        "drq,drx->qx", matching, extra_arrived, preferred_element_type=jnp.float32
    ).astype(jnp.bfloat16)
    by_degree = by_degree.at[:, top].set(
        jnp.where(row_found[:, None], extra_column, by_degree[:, top])
    )
    second = transform(tables, by_degree, degree_map, angles[1])
    main_back = gather_slots("drcw,cwx->drcx", second, in_dpos, in_alive)
    extra_back = jnp.einsum(
        "drq,qx->drx", matching, second[:, top], preferred_element_type=jnp.float32
    ).astype(jnp.bfloat16)
    main_home, extra_home = (
        lax.all_to_all(main_back, "deg", split_axis=0, concat_axis=0, tiled=True),
        lax.all_to_all(extra_back, "deg", split_axis=0, concat_axis=0, tiled=True),
    )
    by_order = place_slots("drcw,drcx->rwx", main_home, out_opos, out_alive, width)
    home_values = jnp.sum(
        jnp.where(out_found[..., None], extra_home.astype(jnp.float32), 0.0), axis=0
    ).astype(jnp.bfloat16)
    home_found = jnp.any(out_found, axis=0)
    home_mask = (position == extra_places[:, None]) & home_found[:, None]
    by_order = jnp.where(home_mask[..., None], home_values[:, None, :], by_order)
    return rotate_phase(by_order, order_map, angles[0])


VMEM = pl.BlockSpec(memory_space=pltpu.VMEM)
SMEM = pl.BlockSpec(memory_space=pltpu.SMEM)
ANY = pl.BlockSpec(memory_space=pl.ANY)
MESH = pl.DeviceIdType.MESH
F32 = jnp.float32
BF16 = jnp.bfloat16
HALF = 8
EACH = 4
SLAB = 32
AHEAD = 4
PLANE = 8


def onehot(a, b):
    return jnp.where(a == b, 1.0, 0.0)


def rotate(v, cosine, sine):
    return v * cosine + pltpu.roll(v, v.shape[-1] // 2, v.ndim - 1) * sine


def dot(a, b):
    return jnp.dot(a, b, preferred_element_type=F32)


def iota(shape, dim):
    return lax.broadcasted_iota(jnp.int32, shape, dim)


def lows(orders):
    shape = (len(orders), 128)
    low = jnp.zeros(shape, jnp.int32)
    for r, order in enumerate(orders):
        low = jnp.where(iota(shape, 0) == r, order, low)
    return low


def phase(order, angle):
    turn = order.astype(F32) * angle
    sine = jnp.sin(turn)
    return jnp.cos(turn), jnp.where(iota(turn.shape, 1) < 64, sine, -sine)


def turning(low, angle, top):
    return [t for order in (low, top - 1 - low) for t in phase(order, angle)]


def fused_kernel(
    n, local, pairs,
    ord_s, deg_s, ang_s, x_ref, raw_ref, qrow, prow,
    rows_out, tab_ref,
    send, recv, back, home, xs, line, scr0, scr1, mats, tbuf, raw, swap, stage,
    uv, xb, sb, ct, st, cs, extra, eall, last, lall, exb, upper,
    out_s, out_r, bk_s, bk_r, ex_s, ex_r, loc, xsem, rawsem, stsem, tsem, osem,
):
    me = lax.axis_index("deg")
    top = 2 * pairs
    width = top + 1
    deep = xb.shape[0]
    span = local * HALF
    chunks = local // EACH
    lead = line.shape[1] - deep

    def peer_of(i):
        step = lax.div(i, 2) + (n // 2) * lax.rem(i, 2)
        return lax.rem(me + step, n)

    barrier = pltpu.get_barrier_semaphore()

    def greet(i, carry):
        pl.semaphore_signal(
            barrier, inc=1, device_id={"deg": lax.rem(me + i, n)}, device_id_type=MESH
        )
        return carry

    lax.fori_loop(1, n, greet, 0)

    def fetch_x(h):
        return pltpu.make_async_copy(
            x_ref.at[:, pl.ds(h * HALF, HALF), :], xs.at[h], xsem.at[h]
        )

    def fetch_raw(b, slot):
        return pltpu.make_async_copy(
            raw_ref.at[pl.ds(b * SLAB, SLAB)], raw.at[slot], rawsem.at[slot]
        )

    fetch_x(0).start()

    def pushing(src, dst, at, count, h, ssem, rsem, i):
        peer = peer_of(i)
        return pltpu.make_async_remote_copy(
            src_ref=src.at[h, peer, pl.ds(at, count)],
            dst_ref=dst.at[h, me, pl.ds(at, count)],
            send_sem=ssem, recv_sem=rsem, device_id={"deg": peer}, device_id_type=MESH,
        )

    def push(src, dst, k, h, ssem, rsem):
        def one(i, carry):
            pushing(src, dst, k * EACH, EACH, h, ssem, rsem, i).start()
            return carry

        lax.fori_loop(1, n, one, 0)

    def whole(src, dst, k, h, ssem, rsem):
        part = (h, pl.ds(0, n - 1), pl.ds(k * EACH, EACH))
        return pltpu.make_async_remote_copy(
            src_ref=src.at[part], dst_ref=dst.at[part],
            send_sem=ssem, recv_sem=rsem, device_id={"deg": lax.rem(me + 1, n)}, device_id_type=MESH,
        )

    planes = n // PLANE
    my_plane, my_place = lax.div(me, PLANE), lax.rem(me, PLANE)

    def across(every, s, i):
        to = lax.rem(me + i * PLANE, n)
        mine = every.at[my_plane, my_place]
        return pltpu.make_async_remote_copy(
            src_ref=mine, dst_ref=mine, send_sem=ex_s.at[s], recv_sem=ex_r.at[s],
            device_id={"deg": to}, device_id_type=MESH,
        )

    def within(every, s, i):
        to = my_plane * PLANE + lax.rem(my_place + i, PLANE)
        mine = every.at[:, my_place]
        return pltpu.make_async_remote_copy(
            src_ref=mine, dst_ref=mine, send_sem=ex_s.at[s + 1], recv_sem=ex_r.at[s + 1],
            device_id={"deg": to}, device_id_type=MESH,
        )

    def gathered(part, s):
        return pltpu.make_async_remote_copy(
            src_ref=part, dst_ref=part, send_sem=ex_s.at[s], recv_sem=ex_r.at[s],
            device_id={"deg": lax.rem(me + 1, n)}, device_id_type=MESH,
        )

    def across_all(every, s):
        return gathered(every.at[pl.ds(0, planes - 1), 0], s)

    def within_all(every, s):
        return gathered(every.at[:, pl.ds(0, PLANE - 1)], s + 1)

    def spread(every, s, value):
        every[my_plane, my_place] = value
        for i in range(1, planes):
            across(every, s, i).start()

    def spread_on(every, s):
        across_all(every, s).wait_recv()
        for i in range(1, PLANE):
            within(every, s, i).start()

    def push_out(p):
        k, h = lax.div(p, 2), lax.rem(p, 2)
        push(send, recv, k, h, out_s.at[p], out_r.at[p])

    def push_back(k, h):
        p = 2 * k + h
        push(back, home, k, h, bk_s.at[p], bk_r.at[p])

    def back_whole(k, h):
        p = 2 * k + h
        return whole(back, home, k, h, bk_s.at[p], bk_r.at[p])

    def stay(src, dst, h, s):
        return pltpu.make_async_copy(src.at[h, me], dst.at[h, me], loc.at[s])

    level = iota((pairs, pairs), 0)
    mats[0] = onehot(pairs - 1 - level, qrow[...]).T.astype(BF16)
    mats[1] = onehot(level, qrow[...]).T.astype(BF16)
    my_lows = lows([ord_s[me * local + r] for r in range(local)])
    for i, t in enumerate(turning(my_lows, ang_s[2], top)):
        cs[i] = t
    row = iota((pairs, 1), 0)

    def pack(h):
        flat = xs.at[h].reshape(width * HALF, 128)

        def one(r, slot):
            at = h * HALF + r
            p = ord_s[me * local + at]
            cl, sl, ch, sh = (cs[i, pl.ds(at, 1), :] for i in range(4))
            line[slot, lead : lead + width, :] = flat[pl.ds(r, width, stride=HALF), :]

            def load(pos):
                return line[slot, pl.ds(lead + pos, pairs), :]

            low = jnp.where(row >= p, rotate(load(-p), cl, sl), 0.0).astype(BF16)
            mid = rotate(load(pairs - p), cl, sl).astype(BF16)
            high = jnp.where(row >= pairs - p, rotate(load(pairs + 1), ch, sh), 0.0).astype(BF16)
            both = dot(mats[0], jnp.concatenate([mid, high], 1))
            extra[pl.ds(at, 1), :] = rotate(line[slot, pl.ds(lead + top - p, 1), :], ch, sh)
            return low, both

        def step(i, carry):
            for r in range(0, AHEAD, 2):
                at = AHEAD * i + r
                low_a, both_a = one(at, r)
                low_b, both_b = one(at + 1, r + 1)
                both_low = dot(mats[1], jnp.concatenate([low_a, low_b], 1))
                for s, both in enumerate((both_a, both_b)):
                    low = both_low[:, s * 128 : (s + 1) * 128]
                    scr0[pl.ds(at + s, pairs, stride=HALF), :] = both[:, :128]
                    scr1[pl.ds(at + s, pairs, stride=HALF), :] = both[:, 128:] + low
            return carry

        lax.fori_loop(0, HALF // AHEAD, step, 0)

        def emit(d, carry):
            at = pl.multiple_of(d * span, 8)
            v0 = scr0[pl.ds(at, span), :].reshape(local, HALF, 128)
            v1 = scr1[pl.ds(at, span), :].reshape(local, HALF, 128)
            send[h, d] = jnp.concatenate([v0, v1], 1).astype(BF16)
            return carry

        lax.fori_loop(0, n, emit, 0)

    fetch_x(0).wait()
    fetch_x(1).start()
    pack(0)
    pl.semaphore_wait(barrier, n - 1)
    push_out(0)
    stay(send, recv, 0, 0).start()
    fetch_x(1).wait()
    fetch_raw(0, 0).start()
    pack(1)
    push_out(1)
    stay(send, recv, 1, 1).start()
    spread(eall, 0, extra[...].astype(BF16))
    push_out(2)

    slabs = top // SLAB
    tall = (local * local, local * local)
    flipped = lax.rem(iota(tall, 1), local) * local + lax.div(iota(tall, 1), local)
    swap[...] = onehot(iota(tall, 0), flipped).astype(BF16)

    def store_slab(b, slot):
        return pltpu.make_async_copy(
            stage.at[slot], tab_ref.at[:, pl.ds(pl.multiple_of(b * SLAB, SLAB), SLAB), :], stsem.at[slot]
        )

    def turn_slab(b, carry):
        slot = lax.rem(b, 2)

        @pl.when(b + 1 < slabs)
        def _():
            fetch_raw(b + 1, 1 - slot).start()

        fetch_raw(b, slot).wait()

        @pl.when(b >= 2)
        def _():
            store_slab(b - 2, slot).wait()

        for at in range(0, SLAB, local):
            block = raw[slot, at : at + local].reshape(local * local, width)
            turned = dot(swap[...], block).astype(BF16)
            stage[slot, :, at : at + local, :] = turned.reshape(local, local, width)
        store_slab(b, slot).start()

        @pl.when(b == slabs // 8)
        def _():
            spread_on(eall, 0)

        @pl.when(lax.rem(b, slabs // 4) == slabs // 4 - 1)
        def _():
            push_out(3 + lax.div(b, slabs // 4))

        return carry

    lax.fori_loop(0, slabs, turn_slab, 0)
    end = pltpu.make_async_copy(raw_ref.at[pl.ds(top, 1)], raw.at[0, pl.ds(0, 1)], rawsem.at[0])
    end.start()
    store_slab(slabs - 2, 0).wait()
    end.wait()
    edge = raw[0, 0].astype(F32)
    first_row = iota((16, 1), 0) == 0
    for j in range(local):
        stage[0, j, 0:16, :] = jnp.where(first_row, edge[j : j + 1, :], 0.0).astype(BF16)
    end = pltpu.make_async_copy(stage.at[0, :, pl.ds(0, 16), :], tab_ref.at[:, pl.ds(top, 16), :], stsem.at[0])
    end.start()
    store_slab(slabs - 1, 1).wait()
    end.wait()

    def fetch_table(c, slot):
        return pltpu.make_async_copy(tab_ref.at[c], tbuf.at[slot], tsem.at[slot])

    fetch_table(0, 0).start()
    a0 = onehot(level, prow[...])
    arev = onehot(pairs - 1 - level, prow[...])
    mats[2] = a0.astype(BF16)
    mats[3] = arev.astype(BF16)
    mats[4] = a0.T.astype(BF16)
    mats[5] = arev.T.astype(BF16)

    def tilt(b, carry):
        at = pl.multiple_of(b * 16, 16)
        cosine, sine = phase(at - pairs + iota((16, 128), 0), ang_s[1])
        ct[pl.ds(at, 16), :] = cosine
        st[pl.ds(at, 16), :] = sine
        return carry

    lax.fori_loop(0, ct.shape[0] // 16, tilt, 0)
    for h in range(2):
        stay(send, recv, h, h).wait()
    within_all(eall, 0).wait_recv()

    def degree(c, carry):
        slot = lax.rem(c, 2)
        k = lax.div(c, EACH)
        spot = lax.rem(c, EACH)

        @pl.when(c + 1 < local)
        def _():
            fetch_table(c + 1, 1 - slot).start()

        @pl.when(spot == 0)
        def _():
            for h in range(2):
                p = 2 * k + h
                whole(send, recv, k, h, out_s.at[p], out_r.at[p]).wait_recv()

        q = deg_s[me * local + c]
        x0 = recv[0, :, c].astype(F32)
        x1 = recv[1, :, c].astype(F32)
        in0 = jnp.concatenate([x0[:, :HALF], x1[:, :HALF]], 1).reshape(pairs, 128).astype(BF16)
        in1 = jnp.concatenate([x0[:, HALF:], x1[:, HALF:]], 1).reshape(pairs, 128).astype(BF16)
        u = dot(mats[2], jnp.concatenate([in0, in1], 1))
        v = dot(mats[3], in1)
        uv[pairs : 2 * pairs, :] = u[:, :128]
        uv[2 * pairs : 3 * pairs, :] = v
        pick = onehot(jnp.broadcast_to(prow[...], (16, pairs)), q).astype(BF16)
        e = dot(pick, eall[...].reshape(pairs, 128))
        xb[0:pairs, :] = jnp.where(row <= q, u[:, 128:], uv[pl.ds(pairs - 1 - q, pairs), :]).astype(BF16)
        xb[pairs:top, :] = uv[pl.ds(top - 1 - q, pairs), :].astype(BF16)
        xb[top : top + 16, :] = e.astype(BF16)
        fetch_table(c, slot).wait()
        first = dot(tbuf[slot], xb[0:width, :])
        low = iota((deep, 1), 0) <= q
        cosine = jnp.where(low, ct[pairs : pairs + deep, :], ct[pl.ds(pairs - 1 - q, deep), :])
        sine = jnp.where(low, st[pairs : pairs + deep, :], st[pl.ds(pairs - 1 - q, deep), :])
        xb[...] = rotate(first, cosine, sine).astype(BF16)
        sb[0:deep, :] = dot(tbuf[slot], xb[0:width, :]).astype(BF16).astype(F32)
        f0 = sb[pl.ds(q + 1, pairs), :].astype(BF16)
        f1 = jnp.where(row <= q, sb[0:pairs, :], 0.0).astype(BF16)
        f2 = jnp.where(row < pairs - 1 - q, sb[pl.ds(q + 1 + pairs, pairs), :], 0.0).astype(BF16)
        g = dot(mats[4], jnp.concatenate([f0, f1], 1))
        g0 = g[:, :128].reshape(n, local, 128)
        g1 = (g[:, 128:] + dot(mats[5], f2)).reshape(n, local, 128)
        for h in range(2):
            cut = slice(h * HALF, (h + 1) * HALF)
            back[h, :, c] = jnp.concatenate([g0[:, cut], g1[:, cut]], 1).astype(BF16)
        last[pl.ds(c, 1), :] = sb[top : top + 1, :]

        @pl.when(c == 1)
        def _():
            push_out(7)

        @pl.when(spot == EACH - 1)
        def _():
            push_back(k, 0)

        return carry

    lax.fori_loop(0, local, degree, 0)
    push_back(0, 1)
    spread(lall, 2, last[...].astype(BF16))
    for h in range(2):
        stay(back, home, h, 2 + h).start()
    mats[0] = onehot(pairs - 1 - level, qrow[...]).astype(BF16)
    mats[1] = onehot(level, qrow[...]).astype(BF16)
    for i, t in enumerate(turning(my_lows, ang_s[0], top)):
        cs[i] = t
    spread_on(lall, 2)
    for k in range(3):
        back_whole(k, 0).wait_send()
    push_back(1, 1)
    back_whole(3, 0).wait_send()
    push_back(2, 1)
    within_all(lall, 2).wait_recv()
    mine = onehot(jnp.broadcast_to(my_lows[:, :1], (local, pairs)), qrow[...]).astype(BF16)
    exb[...] = dot(mine, lall[...].reshape(pairs, 128))
    place = pairs + iota((width - pairs, 1), 0)

    def store_half(h):
        return pltpu.make_async_copy(
            xs.at[h], rows_out.at[:, pl.ds(h * HALF, HALF), :], osem.at[h]
        )

    def take(h, k):
        def one(d, carry):
            at = pl.multiple_of(d * span + k * EACH * HALF, 8)
            got = home[h, d, k * EACH : (k + 1) * EACH].astype(F32)
            scr0[pl.ds(at, EACH * HALF), :] = got[:, :HALF].reshape(EACH * HALF, 128)
            scr1[pl.ds(at, EACH * HALF), :] = got[:, HALF:].reshape(EACH * HALF, 128)
            return carry

        lax.fori_loop(0, n, one, 0)

    def unpack(h):
        flat = xs.at[h].reshape(width * HALF, 128)

        def step(i, carry):
            for r in range(0, AHEAD, 2):
                s1s, boths = [], []
                for s in range(2):
                    at = AHEAD * i + r + s
                    s0 = scr0[pl.ds(at, pairs, stride=HALF), :].astype(BF16)
                    s1 = scr1[pl.ds(at, pairs, stride=HALF), :].astype(BF16)
                    s1s.append(s1)
                    boths.append(dot(mats[0], jnp.concatenate([s0, s1], 1)))
                both_low = dot(mats[1], jnp.concatenate(s1s, 1))
                for s, both in enumerate(boths):
                    at = AHEAD * i + r + s
                    j = h * HALF + at
                    p = ord_s[me * local + j]
                    cl, sl, ch, sh = (cs[t, pl.ds(j, 1), :] for t in range(4))
                    line[r + s, 0:pairs, :] = both_low[:, s * 128 : (s + 1) * 128]
                    line[r + s, pairs:top, :] = both[:, :128]
                    upper[r + s, 8 : 8 + pairs, :] = both[:, 128:]
                    flat[pl.ds(at, pairs, stride=HALF), :] = rotate(line[r + s, pl.ds(p, pairs), :], cl, sl)
                    lower = place < top - p
                    value = jnp.where(place == top - p, exb[pl.ds(j, 1), :], upper[r + s, 7 : 8 + pairs, :])
                    value = jnp.where(lower, line[r + s, pl.ds(p + pairs, pairs + 1), :], value)
                    cosine, sine = jnp.where(lower, cl, ch), jnp.where(lower, sl, sh)
                    high = rotate(value, cosine, sine)
                    flat[pl.ds(pairs * HALF + at, pairs + 1, stride=HALF), :] = high
            return carry

        lax.fori_loop(0, HALF // AHEAD, step, 0)
        store_half(h).start()

    for k in range(chunks):
        back_whole(k, 0).wait_recv()
    stay(back, home, 0, 2).wait()
    push_back(3, 1)
    for k in range(chunks):
        take(0, k)
    unpack(0)
    stay(back, home, 1, 3).wait()
    for k in range(chunks):
        back_whole(k, 1).wait_recv()
        take(1, k)
    unpack(1)
    for p in range(2 * chunks):
        whole(send, recv, p // 2, p % 2, out_s.at[p], out_r.at[p]).wait_send()
    for k in range(chunks):
        back_whole(k, 1).wait_send()
    for every, s in ((eall, 0), (lall, 2)):
        across_all(every, s).wait_send()
        within_all(every, s).wait_send()
    for h in range(2):
        store_half(h).wait()


def shards(coeffs_in, tables, order_pairs, degree_pairs, angles):
    local, width, channels = coeffs_in.shape
    top = width - 1
    pairs = top // 2
    if local != 2 * HALF or channels != 128 or pairs % 128:
        return small_shards(coeffs_in, tables, order_pairs, degree_pairs, angles)
    n = lax.axis_size("deg")
    deep = top + 16
    chunks = local // EACH
    standing = jnp.transpose(coeffs_in, (1, 0, 2))
    tables = jnp.transpose(tables, (1, 0, 2))
    wire = pltpu.VMEM((2, n, local, 2 * HALF, 128), BF16)
    small = pltpu.VMEM((local, 128), F32)
    every = pltpu.VMEM((n // PLANE, PLANE, local, 128), BF16)
    sems = lambda count: pltpu.SemaphoreType.DMA((count,))
    by_row, _ = pl.pallas_call(
        functools.partial(fused_kernel, n, local, pairs),
        name="fused",
        out_shape=[
            jax.ShapeDtypeStruct((width, local, 128), F32),
            jax.ShapeDtypeStruct((local, deep, width), BF16),
        ],
        in_specs=[SMEM, SMEM, SMEM, ANY, ANY, VMEM, VMEM],
        out_specs=[ANY, ANY],
        scratch_shapes=[
            wire, wire, wire, wire,
            pltpu.VMEM((2, width, HALF, 128), F32),
            pltpu.VMEM((AHEAD, pairs + deep, 128), F32),
            pltpu.VMEM((pairs * HALF, 128), F32),
            pltpu.VMEM((pairs * HALF, 128), F32),
            pltpu.VMEM((6, pairs, pairs), BF16),
            pltpu.VMEM((2, deep, width), BF16),
            pltpu.VMEM((2, SLAB, local, width), BF16),
            pltpu.VMEM((local * local, local * local), BF16),
            pltpu.VMEM((2, local, SLAB, width), BF16),
            pltpu.VMEM((3 * pairs, 128), F32),
            pltpu.VMEM((deep, 128), BF16),
            pltpu.VMEM((3 * pairs, 128), F32),
            pltpu.VMEM((pairs + deep, 128), F32),
            pltpu.VMEM((pairs + deep, 128), F32),
            pltpu.VMEM((4, local, 128), F32),
            small, every, small, every, small,
            pltpu.VMEM((AHEAD, pairs + 16, 128), F32),
            sems(2 * chunks), sems(2 * chunks), sems(2 * chunks), sems(2 * chunks),
            sems(4), sems(4), sems(4), sems(2), sems(2), sems(2), sems(2), sems(2),
        ],
        compiler_params=pltpu.CompilerParams(
            collective_id=0, has_side_effects=True, vmem_limit_bytes=62 * 1024 * 1024
        ),
    )(order_pairs, degree_pairs, angles, standing, tables, degree_pairs[None, :], order_pairs[None, :])
    return jnp.transpose(by_row, (1, 0, 2))


def solution(mesh):
    return jax.shard_map(
        shards,
        mesh=mesh,
        in_specs=(P(("grp", "deg"), None, None), P("deg", None, None), P(), P(), P()),
        out_specs=P(("grp", "deg"), None, None),
        check_vma=False,
    )
```

```python
import functools

import jax
import jax.numpy as jnp
from jax import lax
from jax.experimental import pallas as pl
from jax.experimental.pallas import tpu as pltpu
from jax.sharding import PartitionSpec as P


def rotate_phase(values, order_map, angle):
    half = values.shape[-1] // 2
    turn = order_map.astype(jnp.float32)[..., None] * angle
    cosine = jnp.cos(turn)
    sine_part = jnp.sin(turn)
    real_part = values[..., :half].astype(jnp.float32)
    imag_part = values[..., half:].astype(jnp.float32)
    return jnp.concatenate(
        [real_part * cosine + imag_part * sine_part, imag_part * cosine - real_part * sine_part], -1
    )


def packed_places(order_low, degree_low, top):
    lower_side = order_low <= degree_low
    order_pos = jnp.stack(
        [
            top - 1 - degree_low - order_low,
            jnp.where(lower_side, degree_low - order_low, top - degree_low),
        ],
        -1,
    )
    degree_pos = jnp.stack(
        [
            degree_low + 1 + order_low,
            jnp.where(lower_side, order_low, top + degree_low - order_low),
        ],
        -1,
    )
    return (order_pos, degree_pos)


def indicator(places, alive, width):
    columns = jnp.arange(width, dtype=jnp.int32)
    return ((places[..., None] == columns) & alive[..., None]).astype(jnp.bfloat16)


def gather_slots(form, source, places, alive):
    width = source.shape[1]
    pieces = []
    for slot in range(places.shape[-1]):
        table = indicator(places[..., slot], alive[..., slot], width)
        pieces.append(
            jnp.einsum(form, table, source, preferred_element_type=jnp.float32).astype(jnp.bfloat16)
        )
    return jnp.stack(pieces, -2)


def place_slots(form, values, places, alive, width):
    total = None
    for slot in range(places.shape[-1]):
        table = indicator(places[..., slot], alive[..., slot], width)
        term = jnp.einsum(form, table, values[..., slot, :], preferred_element_type=jnp.float32)
        total = term if total is None else total + term
    return total.astype(jnp.bfloat16)


def transform(tables, by_degree, degree_map, tilt):
    first_pass = jnp.einsum("jab,jbc->jac", tables, by_degree, preferred_element_type=jnp.float32)
    tilted = rotate_phase(first_pass, degree_map, tilt).astype(jnp.bfloat16)
    second = jnp.einsum("jab,jbc->jac", tables, tilted, preferred_element_type=jnp.float32)
    return second.astype(jnp.bfloat16)


def small_shards(coeffs_in, tables, order_pairs, degree_pairs, angles):
    local_pairs, width, channels = coeffs_in.shape
    top = width - 1
    devices = lax.axis_size("deg")
    device = lax.axis_index("deg")
    my_orders = lax.dynamic_slice_in_dim(order_pairs, device * local_pairs, local_pairs)
    my_degrees = lax.dynamic_slice_in_dim(degree_pairs, device * local_pairs, local_pairs)
    all_orders = order_pairs.reshape(devices, local_pairs)
    all_degrees = degree_pairs.reshape(devices, local_pairs)
    position = jnp.arange(width, dtype=jnp.int32)[None, :]
    order_map = jnp.where(
        position < top - my_orders[:, None], my_orders[:, None], top - 1 - my_orders[:, None]
    )
    degree_map = jnp.where(
        position <= my_degrees[:, None], position, position - my_degrees[:, None] - 1
    )
    turned = rotate_phase(coeffs_in, order_map, angles[2]).astype(jnp.bfloat16)
    grid_shape = (devices, local_pairs, local_pairs)
    outward_orders = jnp.broadcast_to(my_orders[None, :, None], grid_shape)
    outward_degrees = jnp.broadcast_to(all_degrees[:, None, :], grid_shape)
    inward_orders = jnp.broadcast_to(all_orders[:, :, None], grid_shape)
    inward_degrees = jnp.broadcast_to(my_degrees[None, None, :], grid_shape)
    out_opos, out_dpos = packed_places(outward_orders, outward_degrees, top)
    in_opos, in_dpos = packed_places(inward_orders, inward_degrees, top)
    out_alive = jnp.ones(out_opos.shape, jnp.bool_)
    in_alive = jnp.ones(in_dpos.shape, jnp.bool_)
    out_found = jnp.any(outward_degrees == outward_orders, axis=-1)
    in_match = inward_degrees == inward_orders
    in_found = jnp.any(in_match, axis=-1)
    in_choice = jnp.argmax(in_match.astype(jnp.int32), axis=-1)
    degree_rows = jnp.arange(local_pairs, dtype=jnp.int32)
    matching = ((in_choice[..., None] == degree_rows) & in_found[..., None]).astype(jnp.bfloat16)
    row_found = jnp.any((in_choice[..., None] == degree_rows) & in_found[..., None], axis=(0, 1))
    extra_places = top - my_orders
    extra_values = jnp.take_along_axis(turned, extra_places[:, None, None], 1)[:, 0]
    main_send = gather_slots("drcw,rwx->drcx", turned, out_opos, out_alive)
    extra_send = jnp.where(out_found[..., None], extra_values[None], 0)
    main_arrived, extra_arrived = (
        lax.all_to_all(main_send, "deg", split_axis=0, concat_axis=0, tiled=True),
        lax.all_to_all(extra_send, "deg", split_axis=0, concat_axis=0, tiled=True),
    )
    by_degree = place_slots("drcw,drcx->cwx", main_arrived, in_dpos, in_alive, width)
    extra_column = jnp.einsum(
        "drq,drx->qx", matching, extra_arrived, preferred_element_type=jnp.float32
    ).astype(jnp.bfloat16)
    by_degree = by_degree.at[:, top].set(
        jnp.where(row_found[:, None], extra_column, by_degree[:, top])
    )
    second = transform(tables, by_degree, degree_map, angles[1])
    main_back = gather_slots("drcw,cwx->drcx", second, in_dpos, in_alive)
    extra_back = jnp.einsum(
        "drq,qx->drx", matching, second[:, top], preferred_element_type=jnp.float32
    ).astype(jnp.bfloat16)
    main_home, extra_home = (
        lax.all_to_all(main_back, "deg", split_axis=0, concat_axis=0, tiled=True),
        lax.all_to_all(extra_back, "deg", split_axis=0, concat_axis=0, tiled=True),
    )
    by_order = place_slots("drcw,drcx->rwx", main_home, out_opos, out_alive, width)
    home_values = jnp.sum(
        jnp.where(out_found[..., None], extra_home.astype(jnp.float32), 0.0), axis=0
    ).astype(jnp.bfloat16)
    home_found = jnp.any(out_found, axis=0)
    home_mask = (position == extra_places[:, None]) & home_found[:, None]
    by_order = jnp.where(home_mask[..., None], home_values[:, None, :], by_order)
    return rotate_phase(by_order, order_map, angles[0])


VMEM = pl.BlockSpec(memory_space=pltpu.VMEM)
SMEM = pl.BlockSpec(memory_space=pltpu.SMEM)
ANY = pl.BlockSpec(memory_space=pl.ANY)
MESH = pl.DeviceIdType.MESH
F32 = jnp.float32
BF16 = jnp.bfloat16
HALF = 8
EACH = 4
SLAB = 64
AHEAD = 4
PLANE = 8


def onehot(a, b):
    return jnp.where(a == b, 1.0, 0.0)


def rotate(v, cosine, sine):
    return v * cosine + pltpu.roll(v, v.shape[-1] // 2, v.ndim - 1) * sine


def dot(a, b):
    return jnp.dot(a, b, preferred_element_type=F32)


def iota(shape, dim):
    return lax.broadcasted_iota(jnp.int32, shape, dim)


def lows(orders):
    shape = (len(orders), 128)
    low = jnp.zeros(shape, jnp.int32)
    for r, order in enumerate(orders):
        low = jnp.where(iota(shape, 0) == r, order, low)
    return low


def phase(order, angle):
    turn = order.astype(F32) * angle
    sine = jnp.sin(turn)
    return jnp.cos(turn), jnp.where(iota(turn.shape, 1) < 64, sine, -sine)


def turning(low, angle, top):
    return [t for order in (low, top - 1 - low) for t in phase(order, angle)]


def fused_kernel(
    n, local, pairs,
    ord_s, deg_s, ang_s, x_ref, raw_ref, qrow, prow,
    rows_out, tab_ref,
    send, recv, back, home, xs, line, scr0, scr1, mats, tbuf, raw, swap, stage,
    uv, xb, sb, ct, st, cs, extra, eall, last, lall, exb, upper,
    out_s, out_r, bk_s, bk_r, ex_s, ex_r, loc, xsem, rawsem, stsem, tsem, osem,
):
    me = lax.axis_index("deg")
    top = 2 * pairs
    width = top + 1
    deep = xb.shape[0]
    span = local * HALF
    chunks = local // EACH
    lead = line.shape[1] - deep

    def peer_of(i):
        step = lax.div(i, 2) + (n // 2) * lax.rem(i, 2)
        return lax.rem(me + step, n)

    barrier = pltpu.get_barrier_semaphore()

    def greet(i, carry):
        pl.semaphore_signal(
            barrier, inc=1, device_id={"deg": lax.rem(me + i, n)}, device_id_type=MESH
        )
        return carry

    lax.fori_loop(1, n, greet, 0)

    def fetch_x(h):
        return pltpu.make_async_copy(
            x_ref.at[:, pl.ds(h * HALF, HALF), :], xs.at[h], xsem.at[h]
        )

    def fetch_raw(b, slot):
        return pltpu.make_async_copy(
            raw_ref.at[pl.ds(b * SLAB, SLAB)], raw.at[slot], rawsem.at[slot]
        )

    fetch_x(0).start()

    def pushing(src, dst, at, count, h, ssem, rsem, i):
        peer = peer_of(i)
        return pltpu.make_async_remote_copy(
            src_ref=src.at[h, peer, pl.ds(at, count)],
            dst_ref=dst.at[h, me, pl.ds(at, count)],
            send_sem=ssem, recv_sem=rsem, device_id={"deg": peer}, device_id_type=MESH,
        )

    def push(src, dst, k, h, ssem, rsem):
        def one(i, carry):
            pushing(src, dst, k * EACH, EACH, h, ssem, rsem, i).start()
            return carry

        lax.fori_loop(1, n, one, 0)

    def whole(src, dst, k, h, ssem, rsem):
        part = (h, pl.ds(0, n - 1), pl.ds(k * EACH, EACH))
        return pltpu.make_async_remote_copy(
            src_ref=src.at[part], dst_ref=dst.at[part],
            send_sem=ssem, recv_sem=rsem, device_id={"deg": lax.rem(me + 1, n)}, device_id_type=MESH,
        )

    planes = n // PLANE
    my_plane, my_place = lax.div(me, PLANE), lax.rem(me, PLANE)

    def across(every, s, i):
        to = lax.rem(me + i * PLANE, n)
        mine = every.at[my_plane, my_place]
        return pltpu.make_async_remote_copy(
            src_ref=mine, dst_ref=mine, send_sem=ex_s.at[s], recv_sem=ex_r.at[s],
            device_id={"deg": to}, device_id_type=MESH,
        )

    def within(every, s, i):
        to = my_plane * PLANE + lax.rem(my_place + i, PLANE)
        mine = every.at[:, my_place]
        return pltpu.make_async_remote_copy(
            src_ref=mine, dst_ref=mine, send_sem=ex_s.at[s + 1], recv_sem=ex_r.at[s + 1],
            device_id={"deg": to}, device_id_type=MESH,
        )

    def gathered(part, s):
        return pltpu.make_async_remote_copy(
            src_ref=part, dst_ref=part, send_sem=ex_s.at[s], recv_sem=ex_r.at[s],
            device_id={"deg": lax.rem(me + 1, n)}, device_id_type=MESH,
        )

    def across_all(every, s):
        return gathered(every.at[pl.ds(0, planes - 1), 0], s)

    def within_all(every, s):
        return gathered(every.at[:, pl.ds(0, PLANE - 1)], s + 1)

    def spread(every, s, value):
        every[my_plane, my_place] = value
        for i in range(1, planes):
            across(every, s, i).start()

    def spread_on(every, s):
        across_all(every, s).wait_recv()
        for i in range(1, PLANE):
            within(every, s, i).start()

    def push_out(p):
        k, h = lax.div(p, 2), lax.rem(p, 2)
        push(send, recv, k, h, out_s.at[p], out_r.at[p])

    def push_back(k, h):
        p = 2 * k + h
        push(back, home, k, h, bk_s.at[p], bk_r.at[p])

    def back_whole(k, h):
        p = 2 * k + h
        return whole(back, home, k, h, bk_s.at[p], bk_r.at[p])

    def stay(src, dst, h, s):
        return pltpu.make_async_copy(src.at[h, me], dst.at[h, me], loc.at[s])

    level = iota((pairs, pairs), 0)
    mats[0] = onehot(pairs - 1 - level, qrow[...]).T.astype(BF16)
    mats[1] = onehot(level, qrow[...]).T.astype(BF16)
    my_lows = lows([ord_s[me * local + r] for r in range(local)])
    for i, t in enumerate(turning(my_lows, ang_s[2], top)):
        cs[i] = t
    row = iota((pairs, 1), 0)

    def pack(h):
        flat = xs.at[h].reshape(width * HALF, 128)

        def one(r, slot):
            at = h * HALF + r
            p = ord_s[me * local + at]
            cl, sl, ch, sh = (cs[i, pl.ds(at, 1), :] for i in range(4))
            line[slot, lead : lead + width, :] = flat[pl.ds(r, width, stride=HALF), :]

            def load(pos):
                return line[slot, pl.ds(lead + pos, pairs), :]

            low = jnp.where(row >= p, rotate(load(-p), cl, sl), 0.0).astype(BF16)
            mid = rotate(load(pairs - p), cl, sl).astype(BF16)
            high = jnp.where(row >= pairs - p, rotate(load(pairs + 1), ch, sh), 0.0).astype(BF16)
            both = dot(mats[0], jnp.concatenate([mid, high], 1))
            extra[pl.ds(at, 1), :] = rotate(line[slot, pl.ds(lead + top - p, 1), :], ch, sh)
            return low, both

        def step(i, carry):
            for r in range(0, AHEAD, 2):
                at = AHEAD * i + r
                low_a, both_a = one(at, r)
                low_b, both_b = one(at + 1, r + 1)
                both_low = dot(mats[1], jnp.concatenate([low_a, low_b], 1))
                for s, both in enumerate((both_a, both_b)):
                    low = both_low[:, s * 128 : (s + 1) * 128]
                    scr0[pl.ds(at + s, pairs, stride=HALF), :] = both[:, :128]
                    scr1[pl.ds(at + s, pairs, stride=HALF), :] = both[:, 128:] + low
            return carry

        lax.fori_loop(0, HALF // AHEAD, step, 0)

        def emit(d, carry):
            at = pl.multiple_of(d * span, 8)
            v0 = scr0[pl.ds(at, span), :].reshape(local, HALF, 128)
            v1 = scr1[pl.ds(at, span), :].reshape(local, HALF, 128)
            send[h, d] = jnp.concatenate([v0, v1], 1).astype(BF16)
            return carry

        lax.fori_loop(0, n, emit, 0)

    fetch_x(0).wait()
    fetch_x(1).start()
    pack(0)
    pl.semaphore_wait(barrier, n - 1)
    push_out(0)
    stay(send, recv, 0, 0).start()
    fetch_x(1).wait()
    fetch_raw(0, 0).start()
    pack(1)
    push_out(1)
    stay(send, recv, 1, 1).start()
    spread(eall, 0, extra[...].astype(BF16))
    push_out(2)

    slabs = top // SLAB
    tall = (local * local, local * local)
    flipped = lax.rem(iota(tall, 1), local) * local + lax.div(iota(tall, 1), local)
    swap[...] = onehot(iota(tall, 0), flipped).astype(BF16)

    def store_slab(b, slot):
        return pltpu.make_async_copy(
            stage.at[slot], tab_ref.at[:, pl.ds(pl.multiple_of(b * SLAB, SLAB), SLAB), :], stsem.at[slot]
        )

    def turn_slab(b, carry):
        slot = lax.rem(b, 2)

        @pl.when(b + 1 < slabs)
        def _():
            fetch_raw(b + 1, 1 - slot).start()

        fetch_raw(b, slot).wait()

        @pl.when(b >= 2)
        def _():
            store_slab(b - 2, slot).wait()

        for at in range(0, SLAB, local):
            block = raw[slot, at : at + local].reshape(local * local, width)
            turned = dot(swap[...], block).astype(BF16)
            stage[slot, :, at : at + local, :] = turned.reshape(local, local, width)
        store_slab(b, slot).start()

        @pl.when(b == slabs // 8)
        def _():
            spread_on(eall, 0)

        @pl.when(lax.rem(b, slabs // 4) == slabs // 4 - 1)
        def _():
            push_out(3 + lax.div(b, slabs // 4))

        return carry

    lax.fori_loop(0, slabs, turn_slab, 0)
    end = pltpu.make_async_copy(raw_ref.at[pl.ds(top, 1)], raw.at[0, pl.ds(0, 1)], rawsem.at[0])
    end.start()
    store_slab(slabs - 2, 0).wait()
    end.wait()
    edge = raw[0, 0].astype(F32)
    first_row = iota((16, 1), 0) == 0
    for j in range(local):
        stage[0, j, 0:16, :] = jnp.where(first_row, edge[j : j + 1, :], 0.0).astype(BF16)
    end = pltpu.make_async_copy(stage.at[0, :, pl.ds(0, 16), :], tab_ref.at[:, pl.ds(top, 16), :], stsem.at[0])
    end.start()
    store_slab(slabs - 1, 1).wait()
    end.wait()

    def fetch_table(c, slot):
        return pltpu.make_async_copy(tab_ref.at[c], tbuf.at[slot], tsem.at[slot])

    fetch_table(0, 0).start()
    a0 = onehot(level, prow[...])
    arev = onehot(pairs - 1 - level, prow[...])
    mats[2] = a0.astype(BF16)
    mats[3] = arev.astype(BF16)
    mats[4] = a0.T.astype(BF16)
    mats[5] = arev.T.astype(BF16)

    def tilt(b, carry):
        at = pl.multiple_of(b * 16, 16)
        cosine, sine = phase(at - pairs + iota((16, 128), 0), ang_s[1])
        ct[pl.ds(at, 16), :] = cosine
        st[pl.ds(at, 16), :] = sine
        return carry

    lax.fori_loop(0, ct.shape[0] // 16, tilt, 0)
    for h in range(2):
        stay(send, recv, h, h).wait()
    within_all(eall, 0).wait_recv()

    def degree(c, carry):
        slot = lax.rem(c, 2)
        k = lax.div(c, EACH)
        spot = lax.rem(c, EACH)

        @pl.when(c + 1 < local)
        def _():
            fetch_table(c + 1, 1 - slot).start()

        @pl.when(spot == 0)
        def _():
            for h in range(2):
                p = 2 * k + h
                whole(send, recv, k, h, out_s.at[p], out_r.at[p]).wait_recv()

        q = deg_s[me * local + c]
        x0 = recv[0, :, c].astype(F32)
        x1 = recv[1, :, c].astype(F32)
        in0 = jnp.concatenate([x0[:, :HALF], x1[:, :HALF]], 1).reshape(pairs, 128).astype(BF16)
        in1 = jnp.concatenate([x0[:, HALF:], x1[:, HALF:]], 1).reshape(pairs, 128).astype(BF16)
        u = dot(mats[2], jnp.concatenate([in0, in1], 1))
        v = dot(mats[3], in1)
        uv[pairs : 2 * pairs, :] = u[:, :128]
        uv[2 * pairs : 3 * pairs, :] = v
        pick = onehot(jnp.broadcast_to(prow[...], (16, pairs)), q).astype(BF16)
        e = dot(pick, eall[...].reshape(pairs, 128))
        xb[0:pairs, :] = jnp.where(row <= q, u[:, 128:], uv[pl.ds(pairs - 1 - q, pairs), :]).astype(BF16)
        xb[pairs:top, :] = uv[pl.ds(top - 1 - q, pairs), :].astype(BF16)
        xb[top : top + 16, :] = e.astype(BF16)
        fetch_table(c, slot).wait()
        first = dot(tbuf[slot], xb[0:width, :])
        low = iota((deep, 1), 0) <= q
        cosine = jnp.where(low, ct[pairs : pairs + deep, :], ct[pl.ds(pairs - 1 - q, deep), :])
        sine = jnp.where(low, st[pairs : pairs + deep, :], st[pl.ds(pairs - 1 - q, deep), :])
        xb[...] = rotate(first, cosine, sine).astype(BF16)
        sb[0:deep, :] = dot(tbuf[slot], xb[0:width, :]).astype(BF16).astype(F32)
        f0 = sb[pl.ds(q + 1, pairs), :].astype(BF16)
        f1 = jnp.where(row <= q, sb[0:pairs, :], 0.0).astype(BF16)
        f2 = jnp.where(row < pairs - 1 - q, sb[pl.ds(q + 1 + pairs, pairs), :], 0.0).astype(BF16)
        g = dot(mats[4], jnp.concatenate([f0, f1], 1))
        g0 = g[:, :128].reshape(n, local, 128)
        g1 = (g[:, 128:] + dot(mats[5], f2)).reshape(n, local, 128)
        for h in range(2):
            cut = slice(h * HALF, (h + 1) * HALF)
            back[h, :, c] = jnp.concatenate([g0[:, cut], g1[:, cut]], 1).astype(BF16)
        last[pl.ds(c, 1), :] = sb[top : top + 1, :]

        @pl.when(c == 1)
        def _():
            push_out(7)

        @pl.when(spot == EACH - 1)
        def _():
            push_back(k, 0)

        return carry

    lax.fori_loop(0, local, degree, 0)
    push_back(0, 1)
    spread(lall, 2, last[...].astype(BF16))
    for h in range(2):
        stay(back, home, h, 2 + h).start()
    mats[0] = onehot(pairs - 1 - level, qrow[...]).astype(BF16)
    mats[1] = onehot(level, qrow[...]).astype(BF16)
    for i, t in enumerate(turning(my_lows, ang_s[0], top)):
        cs[i] = t
    spread_on(lall, 2)
    for k in range(3):
        back_whole(k, 0).wait_send()
    push_back(1, 1)
    back_whole(3, 0).wait_send()
    push_back(2, 1)
    within_all(lall, 2).wait_recv()
    mine = onehot(jnp.broadcast_to(my_lows[:, :1], (local, pairs)), qrow[...]).astype(BF16)
    exb[...] = dot(mine, lall[...].reshape(pairs, 128))
    place = pairs + iota((width - pairs, 1), 0)

    def store_half(h):
        return pltpu.make_async_copy(
            xs.at[h], rows_out.at[:, pl.ds(h * HALF, HALF), :], osem.at[h]
        )

    def take(h, k):
        def one(d, carry):
            at = pl.multiple_of(d * span + k * EACH * HALF, 8)
            got = home[h, d, k * EACH : (k + 1) * EACH].astype(F32)
            scr0[pl.ds(at, EACH * HALF), :] = got[:, :HALF].reshape(EACH * HALF, 128)
            scr1[pl.ds(at, EACH * HALF), :] = got[:, HALF:].reshape(EACH * HALF, 128)
            return carry

        lax.fori_loop(0, n, one, 0)

    def unpack(h):
        flat = xs.at[h].reshape(width * HALF, 128)

        def step(i, carry):
            for r in range(0, AHEAD, 2):
                s1s, boths = [], []
                for s in range(2):
                    at = AHEAD * i + r + s
                    s0 = scr0[pl.ds(at, pairs, stride=HALF), :].astype(BF16)
                    s1 = scr1[pl.ds(at, pairs, stride=HALF), :].astype(BF16)
                    s1s.append(s1)
                    boths.append(dot(mats[0], jnp.concatenate([s0, s1], 1)))
                both_low = dot(mats[1], jnp.concatenate(s1s, 1))
                for s, both in enumerate(boths):
                    at = AHEAD * i + r + s
                    j = h * HALF + at
                    p = ord_s[me * local + j]
                    cl, sl, ch, sh = (cs[t, pl.ds(j, 1), :] for t in range(4))
                    line[r + s, 0:pairs, :] = both_low[:, s * 128 : (s + 1) * 128]
                    line[r + s, pairs:top, :] = both[:, :128]
                    upper[r + s, 8 : 8 + pairs, :] = both[:, 128:]
                    flat[pl.ds(at, pairs, stride=HALF), :] = rotate(line[r + s, pl.ds(p, pairs), :], cl, sl)
                    lower = place < top - p
                    value = jnp.where(place == top - p, exb[pl.ds(j, 1), :], upper[r + s, 7 : 8 + pairs, :])
                    value = jnp.where(lower, line[r + s, pl.ds(p + pairs, pairs + 1), :], value)
                    cosine, sine = jnp.where(lower, cl, ch), jnp.where(lower, sl, sh)
                    high = rotate(value, cosine, sine)
                    flat[pl.ds(pairs * HALF + at, pairs + 1, stride=HALF), :] = high
            return carry

        lax.fori_loop(0, HALF // AHEAD, step, 0)
        store_half(h).start()

    for k in range(chunks):
        back_whole(k, 0).wait_recv()
    stay(back, home, 0, 2).wait()
    push_back(3, 1)
    for k in range(chunks):
        take(0, k)
    unpack(0)
    stay(back, home, 1, 3).wait()
    for k in range(chunks):
        back_whole(k, 1).wait_recv()
        take(1, k)
    unpack(1)
    for p in range(2 * chunks):
        whole(send, recv, p // 2, p % 2, out_s.at[p], out_r.at[p]).wait_send()
    for k in range(chunks):
        back_whole(k, 1).wait_send()
    for every, s in ((eall, 0), (lall, 2)):
        across_all(every, s).wait_send()
        within_all(every, s).wait_send()
    for h in range(2):
        store_half(h).wait()


def shards(coeffs_in, tables, order_pairs, degree_pairs, angles):
    local, width, channels = coeffs_in.shape
    top = width - 1
    pairs = top // 2
    if local != 2 * HALF or channels != 128 or pairs % 128:
        return small_shards(coeffs_in, tables, order_pairs, degree_pairs, angles)
    n = lax.axis_size("deg")
    deep = top + 16
    chunks = local // EACH
    standing = jnp.transpose(coeffs_in, (1, 0, 2))
    tables = jnp.transpose(tables, (1, 0, 2))
    wire = pltpu.VMEM((2, n, local, 2 * HALF, 128), BF16)
    small = pltpu.VMEM((local, 128), F32)
    every = pltpu.VMEM((n // PLANE, PLANE, local, 128), BF16)
    sems = lambda count: pltpu.SemaphoreType.DMA((count,))
    by_row, _ = pl.pallas_call(
        functools.partial(fused_kernel, n, local, pairs),
        name="fused",
        out_shape=[
            jax.ShapeDtypeStruct((width, local, 128), F32),
            jax.ShapeDtypeStruct((local, deep, width), BF16),
        ],
        in_specs=[SMEM, SMEM, SMEM, ANY, ANY, VMEM, VMEM],
        out_specs=[ANY, ANY],
        scratch_shapes=[
            wire, wire, wire, wire,
            pltpu.VMEM((2, width, HALF, 128), F32),
            pltpu.VMEM((AHEAD, pairs + deep, 128), F32),
            pltpu.VMEM((pairs * HALF, 128), F32),
            pltpu.VMEM((pairs * HALF, 128), F32),
            pltpu.VMEM((6, pairs, pairs), BF16),
            pltpu.VMEM((2, deep, width), BF16),
            pltpu.VMEM((2, SLAB, local, width), BF16),
            pltpu.VMEM((local * local, local * local), BF16),
            pltpu.VMEM((2, local, SLAB, width), BF16),
            pltpu.VMEM((3 * pairs, 128), F32),
            pltpu.VMEM((deep, 128), BF16),
            pltpu.VMEM((3 * pairs, 128), F32),
            pltpu.VMEM((pairs + deep, 128), F32),
            pltpu.VMEM((pairs + deep, 128), F32),
            pltpu.VMEM((4, local, 128), F32),
            small, every, small, every, small,
            pltpu.VMEM((AHEAD, pairs + 16, 128), F32),
            sems(2 * chunks), sems(2 * chunks), sems(2 * chunks), sems(2 * chunks),
            sems(4), sems(4), sems(4), sems(2), sems(2), sems(2), sems(2), sems(2),
        ],
        compiler_params=pltpu.CompilerParams(
            collective_id=0, has_side_effects=True, vmem_limit_bytes=62 * 1024 * 1024
        ),
    )(order_pairs, degree_pairs, angles, standing, tables, degree_pairs[None, :], order_pairs[None, :])
    return jnp.transpose(by_row, (1, 0, 2))


def solution(mesh):
    return jax.shard_map(
        shards,
        mesh=mesh,
        in_specs=(P(("grp", "deg"), None, None), P("deg", None, None), P(), P(), P()),
        out_specs=P(("grp", "deg"), None, None),
        check_vma=False,
    )
```

```python
import functools

import jax
import jax.numpy as jnp
from jax import lax
from jax.experimental import pallas as pl
from jax.experimental.pallas import tpu as pltpu
from jax.sharding import PartitionSpec as P


def rotate_phase(values, order_map, angle):
    half = values.shape[-1] // 2
    turn = order_map.astype(jnp.float32)[..., None] * angle
    cosine = jnp.cos(turn)
    sine_part = jnp.sin(turn)
    real_part = values[..., :half].astype(jnp.float32)
    imag_part = values[..., half:].astype(jnp.float32)
    return jnp.concatenate(
        [real_part * cosine + imag_part * sine_part, imag_part * cosine - real_part * sine_part], -1
    )


def packed_places(order_low, degree_low, top):
    lower_side = order_low <= degree_low
    order_pos = jnp.stack(
        [
            top - 1 - degree_low - order_low,
            jnp.where(lower_side, degree_low - order_low, top - degree_low),
        ],
        -1,
    )
    degree_pos = jnp.stack(
        [
            degree_low + 1 + order_low,
            jnp.where(lower_side, order_low, top + degree_low - order_low),
        ],
        -1,
    )
    return (order_pos, degree_pos)


def indicator(places, alive, width):
    columns = jnp.arange(width, dtype=jnp.int32)
    return ((places[..., None] == columns) & alive[..., None]).astype(jnp.bfloat16)


def gather_slots(form, source, places, alive):
    width = source.shape[1]
    pieces = []
    for slot in range(places.shape[-1]):
        table = indicator(places[..., slot], alive[..., slot], width)
        pieces.append(
            jnp.einsum(form, table, source, preferred_element_type=jnp.float32).astype(jnp.bfloat16)
        )
    return jnp.stack(pieces, -2)


def place_slots(form, values, places, alive, width):
    total = None
    for slot in range(places.shape[-1]):
        table = indicator(places[..., slot], alive[..., slot], width)
        term = jnp.einsum(form, table, values[..., slot, :], preferred_element_type=jnp.float32)
        total = term if total is None else total + term
    return total.astype(jnp.bfloat16)


def transform(tables, by_degree, degree_map, tilt):
    first_pass = jnp.einsum("jab,jbc->jac", tables, by_degree, preferred_element_type=jnp.float32)
    tilted = rotate_phase(first_pass, degree_map, tilt).astype(jnp.bfloat16)
    second = jnp.einsum("jab,jbc->jac", tables, tilted, preferred_element_type=jnp.float32)
    return second.astype(jnp.bfloat16)


def small_shards(coeffs_in, tables, order_pairs, degree_pairs, angles):
    local_pairs, width, channels = coeffs_in.shape
    top = width - 1
    devices = lax.axis_size("deg")
    device = lax.axis_index("deg")
    my_orders = lax.dynamic_slice_in_dim(order_pairs, device * local_pairs, local_pairs)
    my_degrees = lax.dynamic_slice_in_dim(degree_pairs, device * local_pairs, local_pairs)
    all_orders = order_pairs.reshape(devices, local_pairs)
    all_degrees = degree_pairs.reshape(devices, local_pairs)
    position = jnp.arange(width, dtype=jnp.int32)[None, :]
    order_map = jnp.where(
        position < top - my_orders[:, None], my_orders[:, None], top - 1 - my_orders[:, None]
    )
    degree_map = jnp.where(
        position <= my_degrees[:, None], position, position - my_degrees[:, None] - 1
    )
    turned = rotate_phase(coeffs_in, order_map, angles[2]).astype(jnp.bfloat16)
    grid_shape = (devices, local_pairs, local_pairs)
    outward_orders = jnp.broadcast_to(my_orders[None, :, None], grid_shape)
    outward_degrees = jnp.broadcast_to(all_degrees[:, None, :], grid_shape)
    inward_orders = jnp.broadcast_to(all_orders[:, :, None], grid_shape)
    inward_degrees = jnp.broadcast_to(my_degrees[None, None, :], grid_shape)
    out_opos, out_dpos = packed_places(outward_orders, outward_degrees, top)
    in_opos, in_dpos = packed_places(inward_orders, inward_degrees, top)
    out_alive = jnp.ones(out_opos.shape, jnp.bool_)
    in_alive = jnp.ones(in_dpos.shape, jnp.bool_)
    out_found = jnp.any(outward_degrees == outward_orders, axis=-1)
    in_match = inward_degrees == inward_orders
    in_found = jnp.any(in_match, axis=-1)
    in_choice = jnp.argmax(in_match.astype(jnp.int32), axis=-1)
    degree_rows = jnp.arange(local_pairs, dtype=jnp.int32)
    matching = ((in_choice[..., None] == degree_rows) & in_found[..., None]).astype(jnp.bfloat16)
    row_found = jnp.any((in_choice[..., None] == degree_rows) & in_found[..., None], axis=(0, 1))
    extra_places = top - my_orders
    extra_values = jnp.take_along_axis(turned, extra_places[:, None, None], 1)[:, 0]
    main_send = gather_slots("drcw,rwx->drcx", turned, out_opos, out_alive)
    extra_send = jnp.where(out_found[..., None], extra_values[None], 0)
    main_arrived, extra_arrived = (
        lax.all_to_all(main_send, "deg", split_axis=0, concat_axis=0, tiled=True),
        lax.all_to_all(extra_send, "deg", split_axis=0, concat_axis=0, tiled=True),
    )
    by_degree = place_slots("drcw,drcx->cwx", main_arrived, in_dpos, in_alive, width)
    extra_column = jnp.einsum(
        "drq,drx->qx", matching, extra_arrived, preferred_element_type=jnp.float32
    ).astype(jnp.bfloat16)
    by_degree = by_degree.at[:, top].set(
        jnp.where(row_found[:, None], extra_column, by_degree[:, top])
    )
    second = transform(tables, by_degree, degree_map, angles[1])
    main_back = gather_slots("drcw,cwx->drcx", second, in_dpos, in_alive)
    extra_back = jnp.einsum(
        "drq,qx->drx", matching, second[:, top], preferred_element_type=jnp.float32
    ).astype(jnp.bfloat16)
    main_home, extra_home = (
        lax.all_to_all(main_back, "deg", split_axis=0, concat_axis=0, tiled=True),
        lax.all_to_all(extra_back, "deg", split_axis=0, concat_axis=0, tiled=True),
    )
    by_order = place_slots("drcw,drcx->rwx", main_home, out_opos, out_alive, width)
    home_values = jnp.sum(
        jnp.where(out_found[..., None], extra_home.astype(jnp.float32), 0.0), axis=0
    ).astype(jnp.bfloat16)
    home_found = jnp.any(out_found, axis=0)
    home_mask = (position == extra_places[:, None]) & home_found[:, None]
    by_order = jnp.where(home_mask[..., None], home_values[:, None, :], by_order)
    return rotate_phase(by_order, order_map, angles[0])


VMEM = pl.BlockSpec(memory_space=pltpu.VMEM)
SMEM = pl.BlockSpec(memory_space=pltpu.SMEM)
ANY = pl.BlockSpec(memory_space=pl.ANY)
MESH = pl.DeviceIdType.MESH
F32 = jnp.float32
BF16 = jnp.bfloat16
HALF = 8
EACH = 4
SLAB = 64
AHEAD = 4
PLANE = 8


def onehot(a, b):
    return jnp.where(a == b, 1.0, 0.0)


def rotate(v, cosine, sine):
    return v * cosine + pltpu.roll(v, v.shape[-1] // 2, v.ndim - 1) * sine


def dot(a, b):
    return jnp.dot(a, b, preferred_element_type=F32)


def iota(shape, dim):
    return lax.broadcasted_iota(jnp.int32, shape, dim)


def lows(orders):
    shape = (len(orders), 128)
    low = jnp.zeros(shape, jnp.int32)
    for r, order in enumerate(orders):
        low = jnp.where(iota(shape, 0) == r, order, low)
    return low


def phase(order, angle):
    turn = order.astype(F32) * angle
    sine = jnp.sin(turn)
    return jnp.cos(turn), jnp.where(iota(turn.shape, 1) < 64, sine, -sine)


def turning(low, angle, top):
    return [t for order in (low, top - 1 - low) for t in phase(order, angle)]


def fused_kernel(
    n, local, pairs,
    ord_s, deg_s, ang_s, x_ref, raw_ref, qrow, prow,
    rows_out, tab_ref,
    send, recv, back, home, xs, line, scr0, scr1, mats, tbuf, raw, swap, stage,
    uv, xb, sb, ct, st, cs, extra, eall, last, lall, exb, upper,
    out_s, out_r, bk_s, bk_r, ex_s, ex_r, loc, xsem, rawsem, stsem, tsem, osem,
):
    me = lax.axis_index("deg")
    top = 2 * pairs
    width = top + 1
    deep = xb.shape[0]
    span = local * HALF
    chunks = local // EACH
    lead = line.shape[1] - deep

    def peer_of(i):
        step = lax.div(i, 2) + (n // 2) * lax.rem(i, 2)
        return lax.rem(me + step, n)

    def fetch_x(h):
        return pltpu.make_async_copy(
            x_ref.at[:, pl.ds(h * HALF, HALF), :], xs.at[h], xsem.at[h]
        )

    fetch_x(0).start()
    barrier = pltpu.get_barrier_semaphore()

    def greet(i, carry):
        pl.semaphore_signal(
            barrier, inc=1, device_id={"deg": lax.rem(me + i, n)}, device_id_type=MESH
        )
        return carry

    lax.fori_loop(1, n, greet, 0)

    def fetch_raw(b, slot):
        return pltpu.make_async_copy(
            raw_ref.at[pl.ds(b * SLAB, SLAB)], raw.at[slot], rawsem.at[slot]
        )


    def pushing(src, dst, at, count, h, ssem, rsem, i):
        peer = peer_of(i)
        return pltpu.make_async_remote_copy(
            src_ref=src.at[h, peer, pl.ds(at, count)],
            dst_ref=dst.at[h, me, pl.ds(at, count)],
            send_sem=ssem, recv_sem=rsem, device_id={"deg": peer}, device_id_type=MESH,
        )

    def push(src, dst, k, h, ssem, rsem):
        def one(i, carry):
            pushing(src, dst, k * EACH, EACH, h, ssem, rsem, i).start()
            return carry

        lax.fori_loop(1, n, one, 0)

    def whole(src, dst, k, h, ssem, rsem):
        part = (h, pl.ds(0, n - 1), pl.ds(k * EACH, EACH))
        return pltpu.make_async_remote_copy(
            src_ref=src.at[part], dst_ref=dst.at[part],
            send_sem=ssem, recv_sem=rsem, device_id={"deg": lax.rem(me + 1, n)}, device_id_type=MESH,
        )

    planes = n // PLANE
    my_plane, my_place = lax.div(me, PLANE), lax.rem(me, PLANE)

    def across(every, s, i):
        to = lax.rem(me + i * PLANE, n)
        mine = every.at[my_plane, my_place]
        return pltpu.make_async_remote_copy(
            src_ref=mine, dst_ref=mine, send_sem=ex_s.at[s], recv_sem=ex_r.at[s],
            device_id={"deg": to}, device_id_type=MESH,
        )

    def within(every, s, i):
        to = my_plane * PLANE + lax.rem(my_place + i, PLANE)
        mine = every.at[:, my_place]
        return pltpu.make_async_remote_copy(
            src_ref=mine, dst_ref=mine, send_sem=ex_s.at[s + 1], recv_sem=ex_r.at[s + 1],
            device_id={"deg": to}, device_id_type=MESH,
        )

    def gathered(part, s):
        return pltpu.make_async_remote_copy(
            src_ref=part, dst_ref=part, send_sem=ex_s.at[s], recv_sem=ex_r.at[s],
            device_id={"deg": lax.rem(me + 1, n)}, device_id_type=MESH,
        )

    def across_all(every, s):
        return gathered(every.at[pl.ds(0, planes - 1), 0], s)

    def within_all(every, s):
        return gathered(every.at[:, pl.ds(0, PLANE - 1)], s + 1)

    def spread(every, s, value):
        every[my_plane, my_place] = value
        for i in range(1, planes):
            across(every, s, i).start()

    def spread_on(every, s):
        across_all(every, s).wait_recv()
        for i in range(1, PLANE):
            within(every, s, i).start()

    def push_out(p):
        k, h = lax.div(p, 2), lax.rem(p, 2)
        push(send, recv, k, h, out_s.at[p], out_r.at[p])

    def push_back(k, h):
        p = 2 * k + h
        push(back, home, k, h, bk_s.at[p], bk_r.at[p])

    def back_whole(k, h):
        p = 2 * k + h
        return whole(back, home, k, h, bk_s.at[p], bk_r.at[p])

    def stay(src, dst, h, s):
        return pltpu.make_async_copy(src.at[h, me], dst.at[h, me], loc.at[s])

    level = iota((pairs, pairs), 0)
    mats[0] = onehot(pairs - 1 - level, qrow[...]).T.astype(BF16)
    mats[1] = onehot(level, qrow[...]).T.astype(BF16)
    my_lows = lows([ord_s[me * local + r] for r in range(local)])
    for i, t in enumerate(turning(my_lows, ang_s[2], top)):
        cs[i] = t
    row = iota((pairs, 1), 0)

    def pack(h):
        flat = xs.at[h].reshape(width * HALF, 128)

        def one(r, slot):
            at = h * HALF + r
            p = ord_s[me * local + at]
            cl, sl, ch, sh = (cs[i, pl.ds(at, 1), :] for i in range(4))
            line[slot, lead : lead + width, :] = flat[pl.ds(r, width, stride=HALF), :]

            def load(pos):
                return line[slot, pl.ds(lead + pos, pairs), :]

            low = jnp.where(row >= p, rotate(load(-p), cl, sl), 0.0).astype(BF16)
            mid = rotate(load(pairs - p), cl, sl).astype(BF16)
            high = jnp.where(row >= pairs - p, rotate(load(pairs + 1), ch, sh), 0.0).astype(BF16)
            both = dot(mats[0], jnp.concatenate([mid, high], 1))
            extra[pl.ds(at, 1), :] = rotate(line[slot, pl.ds(lead + top - p, 1), :], ch, sh)
            return low, both

        def step(i, carry):
            for r in range(0, AHEAD, 2):
                at = AHEAD * i + r
                low_a, both_a = one(at, r)
                low_b, both_b = one(at + 1, r + 1)
                both_low = dot(mats[1], jnp.concatenate([low_a, low_b], 1))
                for s, both in enumerate((both_a, both_b)):
                    low = both_low[:, s * 128 : (s + 1) * 128]
                    scr0[pl.ds(at + s, pairs, stride=HALF), :] = both[:, :128]
                    scr1[pl.ds(at + s, pairs, stride=HALF), :] = both[:, 128:] + low
            return carry

        lax.fori_loop(0, HALF // AHEAD, step, 0)

        def emit(d, carry):
            at = pl.multiple_of(d * span, 8)
            v0 = scr0[pl.ds(at, span), :].reshape(local, HALF, 128)
            v1 = scr1[pl.ds(at, span), :].reshape(local, HALF, 128)
            send[h, d] = jnp.concatenate([v0, v1], 1).astype(BF16)
            return carry

        lax.fori_loop(0, n, emit, 0)

    fetch_x(0).wait()
    fetch_x(1).start()
    pack(0)
    pl.semaphore_wait(barrier, n - 1)
    push_out(0)
    stay(send, recv, 0, 0).start()
    fetch_x(1).wait()
    fetch_raw(0, 0).start()
    pack(1)
    push_out(1)
    stay(send, recv, 1, 1).start()
    spread(eall, 0, extra[...].astype(BF16))
    push_out(2)

    slabs = top // SLAB
    tall = (local * local, local * local)
    flipped = lax.rem(iota(tall, 1), local) * local + lax.div(iota(tall, 1), local)
    swap[...] = onehot(iota(tall, 0), flipped).astype(BF16)

    def store_slab(b, slot):
        return pltpu.make_async_copy(
            stage.at[slot], tab_ref.at[:, pl.ds(pl.multiple_of(b * SLAB, SLAB), SLAB), :], stsem.at[slot]
        )

    def turn_slab(b, carry):
        slot = lax.rem(b, 2)

        @pl.when(b + 1 < slabs)
        def _():
            fetch_raw(b + 1, 1 - slot).start()

        fetch_raw(b, slot).wait()

        @pl.when(b >= 2)
        def _():
            store_slab(b - 2, slot).wait()

        for at in range(0, SLAB, local):
            block = raw[slot, at : at + local].reshape(local * local, width)
            turned = dot(swap[...], block).astype(BF16)
            stage[slot, :, at : at + local, :] = turned.reshape(local, local, width)
        store_slab(b, slot).start()

        @pl.when(b == slabs // 8)
        def _():
            spread_on(eall, 0)

        @pl.when(lax.rem(b, slabs // 4) == slabs // 4 - 1)
        def _():
            push_out(3 + lax.div(b, slabs // 4))

        return carry

    lax.fori_loop(0, slabs, turn_slab, 0)
    end = pltpu.make_async_copy(raw_ref.at[pl.ds(top, 1)], raw.at[0, pl.ds(0, 1)], rawsem.at[0])
    end.start()
    store_slab(slabs - 2, 0).wait()
    end.wait()
    edge = raw[0, 0].astype(F32)
    first_row = iota((16, 1), 0) == 0
    for j in range(local):
        stage[0, j, 0:16, :] = jnp.where(first_row, edge[j : j + 1, :], 0.0).astype(BF16)
    end = pltpu.make_async_copy(stage.at[0, :, pl.ds(0, 16), :], tab_ref.at[:, pl.ds(top, 16), :], stsem.at[0])
    end.start()
    store_slab(slabs - 1, 1).wait()
    end.wait()

    def fetch_table(c, slot):
        return pltpu.make_async_copy(tab_ref.at[c], tbuf.at[slot], tsem.at[slot])

    fetch_table(0, 0).start()
    a0 = onehot(level, prow[...])
    arev = onehot(pairs - 1 - level, prow[...])
    mats[2] = a0.astype(BF16)
    mats[3] = arev.astype(BF16)
    mats[4] = a0.T.astype(BF16)
    mats[5] = arev.T.astype(BF16)

    def tilt(b, carry):
        at = pl.multiple_of(b * 16, 16)
        cosine, sine = phase(at - pairs + iota((16, 128), 0), ang_s[1])
        ct[pl.ds(at, 16), :] = cosine
        st[pl.ds(at, 16), :] = sine
        return carry

    lax.fori_loop(0, ct.shape[0] // 16, tilt, 0)
    for h in range(2):
        stay(send, recv, h, h).wait()
    within_all(eall, 0).wait_recv()

    def degree(c, carry):
        slot = lax.rem(c, 2)
        k = lax.div(c, EACH)
        spot = lax.rem(c, EACH)

        @pl.when(c + 1 < local)
        def _():
            fetch_table(c + 1, 1 - slot).start()

        @pl.when(spot == 0)
        def _():
            for h in range(2):
                p = 2 * k + h
                whole(send, recv, k, h, out_s.at[p], out_r.at[p]).wait_recv()

        q = deg_s[me * local + c]
        x0 = recv[0, :, c].astype(F32)
        x1 = recv[1, :, c].astype(F32)
        in0 = jnp.concatenate([x0[:, :HALF], x1[:, :HALF]], 1).reshape(pairs, 128).astype(BF16)
        in1 = jnp.concatenate([x0[:, HALF:], x1[:, HALF:]], 1).reshape(pairs, 128).astype(BF16)
        u = dot(mats[2], jnp.concatenate([in0, in1], 1))
        v = dot(mats[3], in1)
        uv[pairs : 2 * pairs, :] = u[:, :128]
        uv[2 * pairs : 3 * pairs, :] = v
        pick = onehot(jnp.broadcast_to(prow[...], (16, pairs)), q).astype(BF16)
        e = dot(pick, eall[...].reshape(pairs, 128))
        xb[0:pairs, :] = jnp.where(row <= q, u[:, 128:], uv[pl.ds(pairs - 1 - q, pairs), :]).astype(BF16)
        xb[pairs:top, :] = uv[pl.ds(top - 1 - q, pairs), :].astype(BF16)
        xb[top : top + 16, :] = e.astype(BF16)
        fetch_table(c, slot).wait()
        first = dot(tbuf[slot], xb[0:width, :])
        low = iota((deep, 1), 0) <= q
        cosine = jnp.where(low, ct[pairs : pairs + deep, :], ct[pl.ds(pairs - 1 - q, deep), :])
        sine = jnp.where(low, st[pairs : pairs + deep, :], st[pl.ds(pairs - 1 - q, deep), :])
        xb[...] = rotate(first, cosine, sine).astype(BF16)
        sb[0:deep, :] = dot(tbuf[slot], xb[0:width, :]).astype(BF16).astype(F32)
        f0 = sb[pl.ds(q + 1, pairs), :].astype(BF16)
        f1 = jnp.where(row <= q, sb[0:pairs, :], 0.0).astype(BF16)
        f2 = jnp.where(row < pairs - 1 - q, sb[pl.ds(q + 1 + pairs, pairs), :], 0.0).astype(BF16)
        g = dot(mats[4], jnp.concatenate([f0, f1], 1))
        g0 = g[:, :128].reshape(n, local, 128)
        g1 = (g[:, 128:] + dot(mats[5], f2)).reshape(n, local, 128)
        for h in range(2):
            cut = slice(h * HALF, (h + 1) * HALF)
            back[h, :, c] = jnp.concatenate([g0[:, cut], g1[:, cut]], 1).astype(BF16)
        last[pl.ds(c, 1), :] = sb[top : top + 1, :]

        @pl.when(c == 1)
        def _():
            push_out(7)

        @pl.when(spot == EACH - 1)
        def _():
            push_back(k, 0)

            @pl.when(k < chunks - 1)
            def _():
                push_back(k, 1)

        return carry

    lax.fori_loop(0, local, degree, 0)
    spread(lall, 2, last[...].astype(BF16))
    for h in range(2):
        stay(back, home, h, 2 + h).start()
    mats[0] = onehot(pairs - 1 - level, qrow[...]).astype(BF16)
    mats[1] = onehot(level, qrow[...]).astype(BF16)
    for i, t in enumerate(turning(my_lows, ang_s[0], top)):
        cs[i] = t
    spread_on(lall, 2)
    for h in range(2):
        for k in range(chunks - 1):
            back_whole(k, h).wait_send()
    push_back(chunks - 1, 1)
    back_whole(chunks - 1, 0).wait_send()
    within_all(lall, 2).wait_recv()
    mine = onehot(jnp.broadcast_to(my_lows[:, :1], (local, pairs)), qrow[...]).astype(BF16)
    exb[...] = dot(mine, lall[...].reshape(pairs, 128))
    place = pairs + iota((width - pairs, 1), 0)

    def store_half(h):
        return pltpu.make_async_copy(
            xs.at[h], rows_out.at[:, pl.ds(h * HALF, HALF), :], osem.at[h]
        )

    def take(h, k):
        def one(d, carry):
            at = pl.multiple_of(d * span + k * EACH * HALF, 8)
            got = home[h, d, k * EACH : (k + 1) * EACH].astype(F32)
            scr0[pl.ds(at, EACH * HALF), :] = got[:, :HALF].reshape(EACH * HALF, 128)
            scr1[pl.ds(at, EACH * HALF), :] = got[:, HALF:].reshape(EACH * HALF, 128)
            return carry

        lax.fori_loop(0, n, one, 0)

    def unpack(h):
        flat = xs.at[h].reshape(width * HALF, 128)

        def step(i, carry):
            for r in range(0, AHEAD, 2):
                s1s, boths = [], []
                for s in range(2):
                    at = AHEAD * i + r + s
                    s0 = scr0[pl.ds(at, pairs, stride=HALF), :].astype(BF16)
                    s1 = scr1[pl.ds(at, pairs, stride=HALF), :].astype(BF16)
                    s1s.append(s1)
                    boths.append(dot(mats[0], jnp.concatenate([s0, s1], 1)))
                both_low = dot(mats[1], jnp.concatenate(s1s, 1))
                for s, both in enumerate(boths):
                    at = AHEAD * i + r + s
                    j = h * HALF + at
                    p = ord_s[me * local + j]
                    cl, sl, ch, sh = (cs[t, pl.ds(j, 1), :] for t in range(4))
                    line[r + s, 0:pairs, :] = both_low[:, s * 128 : (s + 1) * 128]
                    line[r + s, pairs:top, :] = both[:, :128]
                    upper[r + s, 8 : 8 + pairs, :] = both[:, 128:]
                    flat[pl.ds(at, pairs, stride=HALF), :] = rotate(line[r + s, pl.ds(p, pairs), :], cl, sl)
                    lower = place < top - p
                    value = jnp.where(place == top - p, exb[pl.ds(j, 1), :], upper[r + s, 7 : 8 + pairs, :])
                    value = jnp.where(lower, line[r + s, pl.ds(p + pairs, pairs + 1), :], value)
                    cosine, sine = jnp.where(lower, cl, ch), jnp.where(lower, sl, sh)
                    high = rotate(value, cosine, sine)
                    flat[pl.ds(pairs * HALF + at, pairs + 1, stride=HALF), :] = high
            return carry

        lax.fori_loop(0, HALF // AHEAD, step, 0)
        store_half(h).start()

    for k in range(chunks):
        back_whole(k, 0).wait_recv()
    stay(back, home, 0, 2).wait()
    for k in range(chunks):
        take(0, k)
    unpack(0)
    stay(back, home, 1, 3).wait()
    for k in range(chunks):
        back_whole(k, 1).wait_recv()
        take(1, k)
    unpack(1)
    for p in range(2 * chunks):
        whole(send, recv, p // 2, p % 2, out_s.at[p], out_r.at[p]).wait_send()
    back_whole(chunks - 1, 1).wait_send()
    for every, s in ((eall, 0), (lall, 2)):
        across_all(every, s).wait_send()
        within_all(every, s).wait_send()
    for h in range(2):
        store_half(h).wait()


def shards(coeffs_in, tables, order_pairs, degree_pairs, angles):
    local, width, channels = coeffs_in.shape
    top = width - 1
    pairs = top // 2
    if local != 2 * HALF or channels != 128 or pairs % 128:
        return small_shards(coeffs_in, tables, order_pairs, degree_pairs, angles)
    n = lax.axis_size("deg")
    deep = top + 16
    chunks = local // EACH
    standing = jnp.transpose(coeffs_in, (1, 0, 2))
    tables = jnp.transpose(tables, (1, 0, 2))
    wire = pltpu.VMEM((2, n, local, 2 * HALF, 128), BF16)
    small = pltpu.VMEM((local, 128), F32)
    every = pltpu.VMEM((n // PLANE, PLANE, local, 128), BF16)
    sems = lambda count: pltpu.SemaphoreType.DMA((count,))
    by_row, _ = pl.pallas_call(
        functools.partial(fused_kernel, n, local, pairs),
        name="fused",
        out_shape=[
            jax.ShapeDtypeStruct((width, local, 128), F32),
            jax.ShapeDtypeStruct((local, deep, width), BF16),
        ],
        in_specs=[SMEM, SMEM, SMEM, ANY, ANY, VMEM, VMEM],
        out_specs=[ANY, ANY],
        scratch_shapes=[
            wire, wire, wire, wire,
            pltpu.VMEM((2, width, HALF, 128), F32),
            pltpu.VMEM((AHEAD, pairs + deep, 128), F32),
            pltpu.VMEM((pairs * HALF, 128), F32),
            pltpu.VMEM((pairs * HALF, 128), F32),
            pltpu.VMEM((6, pairs, pairs), BF16),
            pltpu.VMEM((2, deep, width), BF16),
            pltpu.VMEM((2, SLAB, local, width), BF16),
            pltpu.VMEM((local * local, local * local), BF16),
            pltpu.VMEM((2, local, SLAB, width), BF16),
            pltpu.VMEM((3 * pairs, 128), F32),
            pltpu.VMEM((deep, 128), BF16),
            pltpu.VMEM((3 * pairs, 128), F32),
            pltpu.VMEM((pairs + deep, 128), F32),
            pltpu.VMEM((pairs + deep, 128), F32),
            pltpu.VMEM((4, local, 128), F32),
            small, every, small, every, small,
            pltpu.VMEM((AHEAD, pairs + 16, 128), F32),
            sems(2 * chunks), sems(2 * chunks), sems(2 * chunks), sems(2 * chunks),
            sems(4), sems(4), sems(4), sems(2), sems(2), sems(2), sems(2), sems(2),
        ],
        compiler_params=pltpu.CompilerParams(
            collective_id=0, has_side_effects=True, vmem_limit_bytes=62 * 1024 * 1024
        ),
    )(order_pairs, degree_pairs, angles, standing, tables, degree_pairs[None, :], order_pairs[None, :])
    return jnp.transpose(by_row, (1, 0, 2))


def solution(mesh):
    return jax.shard_map(
        shards,
        mesh=mesh,
        in_specs=(P(("grp", "deg"), None, None), P("deg", None, None), P(), P(), P()),
        out_specs=P(("grp", "deg"), None, None),
        check_vma=False,
    )
```
